128 devices in a mesh: root: 4 (over z_lo, core), virt: 32 (over z_hi, y, x).
Axes of the slice: x: 4, y: 4, z: 4 (z_hi: 2, z_lo: 2; z = z_hi * 2 + z_lo), core: 2. Of those that a mesh axis runs over, the one named last changes fastest.
Arguments:
- r2: bfloat16 [512, 16384], P('virt', 'root'), parts along dimension 1, may hold values from -6 to 6
- tau: bfloat16 [512, 512, 3072], P('virt', None, 'root'), parts along dimension 2, may hold values from -6 to 6
- w_vvv: bfloat16 [512, 512, 512], P('virt'), may hold values from -0.01171875 to 0.01171875
- w_oooo: bfloat16 [768, 4096], P('virt'), may hold values from -0.09375 to 0.09375
- w_ovoo: bfloat16 [64, 768, 512], P(None, 'virt'), may hold values from -0.75 to 0.75
- fock_oo: bfloat16 [64, 64], replicated, may hold values from -0.75 to 0.75
- fock_vv: bfloat16 [512, 512], replicated, may hold values from -0.25 to 0.25
- r1: bfloat16 [256], P('root'), parts along dimension 0, may hold values from -6 to 6
Outputs:
- sigma: float32 [3072, 512], P(('root', 'virt')), parts along dimension 0
The draws below stay inside these ranges and needn't reach their ends.
There are 4 independent parts, one for each index of `root`. The reference program is written for one: setup_inputs(seed, part) draws one part's arguments, and reference() takes and returns one part's arrays. A program takes and returns all parts, laid end to end along the dimension named above; an argument that names none is the same for every part. Nothing has to cross between parts.
All inputs are finite; a program needn't handle non-finite values.
Results may differ from the reference program's by a relative error of at most 0.0003.
Values may be sent and summed in bfloat16 or wider, within the bound.
A program may use at most 192 MiB of HBM per device.

```python
import jax
import jax.numpy as jnp
from jax import lax

O = 64
V = 512
OI = 12
PAIRS = 768


def spiked(values, stream_key, source, target, blocks, factor):
    owner, partner = [(jnp.arange(values.shape[dim]) // (values.shape[dim] // blocks)).reshape([-1 if axis == dim else 1 for axis in range(values.ndim)]) for dim in (source, target)]
    chosen = jax.random.permutation(stream_key, blocks)[partner]
    strong = (owner == chosen) | (owner == (partner + blocks // 2) % blocks)
    return jnp.where(strong, factor * values, values)


def block_scale(key, extent, split, smallest, high):
    factor_of = 1.0
    for axis_at, blocks in split:
        heights = jax.random.uniform(jax.random.fold_in(jax.random.fold_in(key, 6), axis_at), (blocks,), jnp.float32, smallest / len(split), high / len(split))
        factor_of = factor_of * jnp.repeat(jnp.exp(heights), extent[axis_at] // blocks).reshape((-1,) + (1,) * (len(extent) - 1 - axis_at))
    return factor_of


def noise(own_key, shape, width, bound, cuts=(), kind=jnp.bfloat16):
    entries = jax.random.normal(own_key, shape, jnp.float32) * width
    if len(cuts) > 0:
        entries = block_scale(own_key, shape, cuts, -0.22, 0.18) * entries
    return jnp.clip(entries, min=-bound, max=bound).astype(kind)


def noise_with(key, extent, scale, limit, shards, heavy, dtype=jnp.bfloat16):
    result = scale * jax.random.normal(key, extent, jnp.float32)
    if shards:
        result = result * block_scale(key, extent, shards, -0.22, 0.18)
    return jnp.clip(spiked(result, jax.random.fold_in(key, 3), *heavy), -limit, limit).astype(dtype)


def setup_inputs(seed: int = 0, part: int = 0) -> dict:
    key_of = jax.random.split(jax.random.key(seed), 9)
    part_splits = jax.random.split(jax.random.fold_in(key_of[8], part), 9)
    r2 = noise(part_splits[0], (V, O * O), 1.0, 6.0, ((0, 32),))
    tau = noise_with(part_splits[1], (V, V, PAIRS), 1.0, 6.0, ((0, 32),), (0, 2, 32, 2.75))
    w_vvv = noise(key_of[2], (V, V, V), (V * V) ** -0.5, 0.01171875, ((0, 32),))
    w_oooo = noise(key_of[3], (PAIRS, O * O), (O * O) ** -0.5, 0.09375, ((0, 32),))
    w_ovoo = noise(key_of[4], (O, PAIRS, V), O ** -0.5, 0.75, ((1, 32),))
    fock_oo = noise(key_of[5], (O, O), O ** -0.5, 0.75)
    fock_vv = noise(key_of[6], (V, V), V ** -0.5, 0.25)
    r1 = noise(part_splits[7], (O,), 1.0, 6.0)
    return dict(r2=r2, tau=tau, w_vvv=w_vvv, w_oooo=w_oooo, w_ovoo=w_ovoo, fock_oo=fock_oo, fock_vv=fock_vv, r1=r1)


def reference(r2, tau, w_vvv, w_oooo, w_ovoo, fock_oo, fock_vv, r1):
    pair_count = OI * O
    tau_flat = tau.reshape(V * V, pair_count)
    weight_flat = jnp.transpose(w_vvv, (1, 0, 2)).reshape(V * V, V)
    three_virtual = jnp.dot(tau_flat.T, weight_flat, preferred_element_type=jnp.float32)
    window = r2[:, :pair_count]
    vv_term = jnp.dot(window.T, fock_vv.T, preferred_element_type=jnp.float32)
    oooo_term = jnp.dot(w_oooo, r2.T, preferred_element_type=jnp.float32)
    cubic_view = r2.astype(jnp.float32).reshape(V, O, O)
    fock_wide = fock_oo.astype(jnp.float32)
    first_term = jnp.einsum("mi,amj->aij", fock_wide, cubic_view, precision=lax.Precision.HIGHEST)
    second_term = jnp.einsum("mj,aim->aij", fock_wide, cubic_view, precision=lax.Precision.HIGHEST)
    occ_term = (first_term + second_term).reshape(V, O * O)[:, :pair_count].T
    singles_term = jnp.dot(r1[None, :], w_ovoo.reshape(O, pair_count * V), preferred_element_type=jnp.float32).reshape(pair_count, V)
    return three_virtual + vv_term + oooo_term - occ_term - singles_term
```

```python
import functools
import math

import jax
import jax.numpy as jnp
from jax import lax
from jax.experimental import pallas as pl
from jax.experimental.pallas import tpu as pltpu
from jax.sharding import PartitionSpec as P

MESH = pl.DeviceIdType.MESH
F32, BF16 = jnp.float32, jnp.bfloat16
EB = 16
HALF = 8
LONG = 5
SHARE = 3
SLOTS = 4
LAG = 2


def dot(a, b, ca, cb):
    return lax.dot_general(a, b, (((ca,), (cb,)), ((), ())), preferred_element_type=F32)


def iotas(rows, cols):
    return (lax.broadcasted_iota(jnp.int32, (rows, cols), 0), lax.broadcasted_iota(jnp.int32, (rows, cols), 1))


def onehot(mask):
    return jnp.where(mask, 1.0, 0.0).astype(BF16)


def kernel(
    ny, nx,
    r2, tau, w, wo, wov, foo, fvv, r1,
    out,
    wbuf, tbuf, acc, rbuf, wovb, r2s, wos, foob, fvvb, winb, r1b, sing, perm,
    tau_sem, loc_sem, long_send, long_recv, z_send, z_recv, sib_send, sib_recv, small_send, small_recv, rs_send, rs_recv,
):
    nv = 2 * ny * nx
    nocc = foo.shape[0]
    pairs = tau.shape[2]
    rows = pairs // nv
    cw = wo.shape[1] // nv
    virt = fvv.shape[0]
    ob = int(math.log2(nocc))
    root, me = lax.axis_index("root"), lax.axis_index("virt")
    zl, c = root // 2, root % 2
    zh, y, x = me // (ny * nx), (me // nx) % ny, me % nx
    sibling = (zl * 2 + 1 - c, me)
    partner = ((1 - zl) * 2 + c, me)

    def peer(j, sign):
        k = (j * 13) % nv
        oz, oy, ox = k // (ny * nx), (k // nx) % ny, k % nx
        v = ((zh + oz) % 2) * (ny * nx) + ((y + sign * oy + ny) % ny) * nx + (x + sign * ox + nx) % nx
        return v, (zl + oz) % 2

    def tau_copy(j):
        v, _ = peer(j, -1)
        return pltpu.make_async_copy(
            tau.at[:, pl.ds(pl.multiple_of(v * EB, EB), EB), :], tbuf.at[j % SLOTS], tau_sem.at[j % SLOTS]
        )

    mine = pl.ds(pl.multiple_of(me * EB, EB), EB)
    my_cols = pl.ds(pl.multiple_of(me * cw, cw), cw)
    local = [
        pltpu.make_async_copy(w.at[:, mine, :], wbuf.at[0], loc_sem.at[0]),
        pltpu.make_async_copy(wov, wovb, loc_sem.at[1]),
        pltpu.make_async_copy(foo, foob, loc_sem.at[2]),
        pltpu.make_async_copy(fvv, fvvb, loc_sem.at[3]),
        pltpu.make_async_copy(r2.at[:, pl.ds(0, pairs)], winb, loc_sem.at[4]),
        pltpu.make_async_copy(r2.at[:, my_cols], r2s.at[mine, :], loc_sem.at[5]),
        pltpu.make_async_copy(wo.at[:, my_cols], wos.at[me], loc_sem.at[6]),
        pltpu.make_async_copy(r1, r1b, loc_sem.at[7]),
    ]

    barrier = pltpu.get_barrier_semaphore()

    def greet(j, _):
        v, zd = peer(j, 1)
        pl.semaphore_signal(barrier, inc=1, device_id=(root, v), device_id_type=MESH)

        @pl.when(zd != zl)
        def _():
            pl.semaphore_signal(barrier, inc=1, device_id=(zd * 2 + c, v), device_id_type=MESH)

        return 0

    lax.fori_loop(1, nv, greet, 0)
    for other in (sibling, partner):
        pl.semaphore_signal(barrier, inc=1, device_id=other, device_id_type=MESH)
    for copy in local:
        copy.start()
    for j in range(LAG):
        tau_copy(j).start()
    pl.semaphore_wait(barrier, nv - 1 + nv // 2 + 2)

    def small_copies(v):
        cols = pl.ds(pl.multiple_of(v * cw, cw), cw)
        return (
            pltpu.make_async_remote_copy(
                src_ref=r2.at[:, cols], dst_ref=r2s.at[mine, :], send_sem=small_send.at[0], recv_sem=small_recv.at[0],
                device_id=(root, v), device_id_type=MESH,
            ),
            pltpu.make_async_remote_copy(
                src_ref=wo.at[:, cols], dst_ref=wos.at[me], send_sem=small_send.at[1], recv_sem=small_recv.at[1],
                device_id=(root, v), device_id_type=MESH,
            ),
        )

    def send(j, _):
        v, zd = peer(j, 1)
        first = HALF * c + SHARE * zd
        pltpu.make_async_remote_copy(
            src_ref=w.at[pl.ds(first, LONG), pl.ds(pl.multiple_of(v * EB, EB), EB), :],
            dst_ref=wbuf.at[j, pl.ds(first, LONG)],
            send_sem=long_send.at[0],
            recv_sem=long_recv.at[j],
            device_id=(zd * 2 + c, v),
            device_id_type=MESH,
        ).start()
        for copy in small_copies(v):
            copy.start()
        return 0

    lax.fori_loop(1, nv, send, 0)

    i, j = iotas(EB * EB, EB * EB)
    perm[...] = onehot(((i >> 4) == (j & 15)) & ((i & 15) == (j >> 4)))

    local[3].wait()
    local[4].wait()
    i, j = iotas(EB, virt)
    chosen = dot(onehot(j == i + me * EB), fvvb[...], 1, 1).astype(BF16)
    acc[...] = dot(winb[...], chosen, 0, 0)

    def z_copy(j):
        part = wbuf.at[j, pl.ds(HALF * c + LONG * zl, SHARE)]
        return pltpu.make_async_remote_copy(
            src_ref=part, dst_ref=part, send_sem=z_send.at[0], recv_sem=z_recv.at[j], device_id=partner, device_id_type=MESH
        )

    def sib_copy(j):
        part = wbuf.at[j, pl.ds(HALF * c, HALF)]
        return pltpu.make_async_remote_copy(
            src_ref=part, dst_ref=part, send_sem=sib_send.at[0], recv_sem=sib_recv.at[j], device_id=sibling, device_id_type=MESH
        )

    def received(ref, sem):
        pltpu.make_async_copy(ref, ref, sem).wait()

    def compute(j):
        tau_copy(j).wait()
        block = tbuf[j % SLOTS].reshape(EB * EB, pairs)
        turned = dot(perm[...], block, 1, 0).astype(BF16)
        weights = wbuf[j].reshape(EB * EB, virt)
        step = pairs // 3
        for part in range(3):
            at = slice(part * step, (part + 1) * step)
            acc[at, :] += dot(turned[:, at], weights, 0, 0)

    def advance(j, _):
        @pl.when(j + LAG < nv)
        def _():
            tau_copy(j + LAG).start()

        @pl.when(j + 2 < nv)
        def _():
            received(wbuf.at[j + 2, pl.ds(HALF * c + SHARE * zl, LONG)], long_recv.at[j + 2])
            z_copy(j + 2).start()

        @pl.when((j + 1 < nv) & (j + 1 > 0))
        def _():
            received(wbuf.at[j + 1, pl.ds(HALF * c + LONG * (1 - zl), SHARE)], z_recv.at[j + 1])
            sib_copy(j + 1).start()

        @pl.when(j > 0)
        def _():
            received(wbuf.at[j, pl.ds(HALF * (1 - c), HALF)], sib_recv.at[j])

        compute(j)
        return 0

    received(wbuf.at[1, pl.ds(HALF * c + SHARE * zl, LONG)], long_recv.at[1])
    z_copy(1).start()
    local[0].wait()
    middle = nv // 2
    lax.fori_loop(0, middle, advance, 0)

    local[1].wait()
    local[7].wait()
    i, j = iotas(nocc, nocc)
    spread = jnp.where(i == j, jnp.broadcast_to(r1b[...].astype(F32), (nocc, nocc)), 0.0).astype(BF16)
    winb32 = dot(spread, jnp.ones((nocc, 128), BF16), 1, 0)
    sing[...] = jnp.zeros_like(sing)
    for k in range(nocc):
        factor = jnp.broadcast_to(winb32[k : k + 1, 0:1], (rows, virt))
        sing[...] += factor * wovb[k].astype(F32)

    local[2].wait()
    local[5].wait()
    local[6].wait()
    others = (nv - 1) * EB
    received(r2s.at[pl.ds(0, others), :], small_recv.at[0])
    received(wos.at[pl.ds(0, nv - 1)], small_recv.at[1])
    held = r2s[...]
    fock = foob[...]
    m_first = me * (cw // nocc)
    i, j = iotas(nocc, cw)
    by_i = dot(fock, onehot(i == (j >> ob) + m_first), 0, 0).astype(BF16)
    by_j = dot(fock, onehot(i == (j & (nocc - 1))), 0, 0).astype(BF16)
    p, q = iotas(pairs, nocc)
    take_i = dot(onehot((p >> ob) == q), by_i, 1, 0)
    take_j = dot(onehot((p & (nocc - 1)) == q), by_j, 1, 0)
    p, q = iotas(pairs, cw)
    first = jnp.where((p & (nocc - 1)) == (q & (nocc - 1)), take_i, 0.0).astype(BF16)
    second = jnp.where((p >> ob) == (q >> ob) + m_first, take_j, 0.0).astype(BF16)
    quartic = wos[...].astype(F32).reshape(pairs, cw).astype(BF16)
    acc[...] += dot(quartic, held, 1, 1) - dot(first, held, 1, 1) - dot(second, held, 1, 1)

    lax.fori_loop(middle, nv, advance, 0)

    def share(j, _):
        v, _zd = peer(j, 1)
        pltpu.make_async_remote_copy(
            src_ref=acc.at[pl.ds(pl.multiple_of(v * rows, 8), rows), :],
            dst_ref=rbuf.at[j],
            send_sem=rs_send.at[0],
            recv_sem=rs_recv.at[0],
            device_id=(root, v),
            device_id_type=MESH,
        ).start()
        return 0

    lax.fori_loop(1, nv, share, 0)
    sing[...] = acc[pl.ds(pl.multiple_of(me * rows, 8), rows), :] - sing[...]
    received(wbuf.at[pl.ds(0, nv - 1), pl.ds(0, LONG)], long_send.at[0])
    received(wbuf.at[pl.ds(0, nv - 1), pl.ds(0, SHARE)], z_send.at[0])
    received(wbuf.at[pl.ds(0, nv - 1), pl.ds(0, HALF)], sib_send.at[0])
    received(r2s.at[pl.ds(0, others), :], small_send.at[0])
    received(wos.at[pl.ds(0, nv - 1)], small_send.at[1])
    received(rbuf.at[pl.ds(1, nv - 1)], rs_recv.at[0])
    out[...] = sing[...] + jnp.sum(rbuf[pl.ds(1, nv - 1)], axis=0)
    received(rbuf.at[pl.ds(1, nv - 1)], rs_send.at[0])


def on_device(r2, tau, w, wo, wov, foo, fvv, r1):
    nv = w.shape[1] // w.shape[0]
    side = int(math.isqrt(nv // 2))
    rows, virt, pairs, nocc = wo.shape[0], w.shape[2], tau.shape[2], foo.shape[0]
    cw = wo.shape[1] // nv
    dma = pltpu.SemaphoreType.DMA
    flops = 2 * nv * EB * EB * pairs * (virt + EB * EB)
    return pl.pallas_call(
        functools.partial(kernel, side, side),
        out_shape=jax.ShapeDtypeStruct((rows, virt), F32),
        in_specs=[pl.BlockSpec(memory_space=pl.ANY)] * 8,
        out_specs=pl.BlockSpec(memory_space=pltpu.VMEM),
        scratch_shapes=[
            pltpu.VMEM((nv, EB, EB, virt), BF16),
            pltpu.VMEM((SLOTS, EB, EB, pairs), BF16),
            pltpu.VMEM((pairs, virt), F32),
            pltpu.VMEM((nv, rows, virt), F32),
            pltpu.VMEM((nocc, rows, virt), BF16),
            pltpu.VMEM((virt, cw), BF16),
            pltpu.VMEM((nv, rows, cw), BF16),
            pltpu.VMEM((nocc, nocc), BF16),
            pltpu.VMEM((virt, virt), BF16),
            pltpu.VMEM((EB, pairs), BF16),
            pltpu.VMEM((1, nocc), BF16),
            pltpu.VMEM((rows, virt), F32),
            pltpu.VMEM((EB * EB, EB * EB), BF16),
            dma((SLOTS,)), dma((8,)),
            dma((1,)), dma((nv,)), dma((1,)), dma((nv,)), dma((1,)), dma((nv,)),
            dma((2,)), dma((2,)), dma((1,)), dma((1,)),
        ],
        compiler_params=pltpu.CompilerParams(collective_id=0, has_side_effects=True, vmem_limit_bytes=56 * 2**20),
        cost_estimate=pl.CostEstimate(flops=flops, bytes_accessed=26_000_000, transcendentals=0),
        name="ladder",
    )(r2, tau, w, wo, wov, foo, fvv, r1.reshape(1, -1))


def solution(mesh):
    in_specs = (
        P("virt", "root"),
        P("virt", None, "root"),
        P("virt", None, None),
        P("virt", None),
        P(None, "virt", None),
        P(),
        P(),
        P("root"),
    )
    return jax.shard_map(
        on_device, mesh=mesh, in_specs=in_specs, out_specs=P(("root", "virt"), None), check_vma=False
    )
```

```python
import functools
import math

import jax
import jax.numpy as jnp
from jax import lax
from jax.experimental import pallas as pl
from jax.experimental.pallas import tpu as pltpu
from jax.sharding import PartitionSpec as P

MESH = pl.DeviceIdType.MESH
F32, BF16 = jnp.float32, jnp.bfloat16
EB = 16
HALF = 8
LONG = 5
SHARE = 3
SLOTS = 8
Z_LAG = 3
S_LAG = 3
LAG = Z_LAG + S_LAG


def dot(a, b, ca, cb):
    return lax.dot_general(a, b, (((ca,), (cb,)), ((), ())), preferred_element_type=F32)


def iotas(rows, cols):
    return (lax.broadcasted_iota(jnp.int32, (rows, cols), 0), lax.broadcasted_iota(jnp.int32, (rows, cols), 1))


def onehot(mask):
    return jnp.where(mask, 1.0, 0.0).astype(BF16)


def kernel(
    ny, nx,
    r2, tau, w, wo, wov, foo, fvv, r1,
    out,
    wbuf, tbuf, acc, first_x, first_y, total_x, total_y, last_x, last_y, wovb, r2s, wos, foob, fvvb, winb, r1b, sing, perm,
    tau_sem, loc_sem, long_send, long_recv, z_send, z_recv, sib_send, sib_recv, small_send, small_recv, rs_send, rs_recv,
):
    nv = 2 * ny * nx
    nocc = foo.shape[0]
    pairs = tau.shape[2]
    rows = pairs // nv
    cw = wo.shape[1] // nv
    virt = fvv.shape[0]
    ob = int(math.log2(nocc))
    root, me = lax.axis_index("root"), lax.axis_index("virt")
    zl, c = root // 2, root % 2
    zh, y, x = me // (ny * nx), (me // nx) % ny, me % nx
    sibling = (zl * 2 + 1 - c, me)
    partner = ((1 - zl) * 2 + c, me)

    def peer(j, sign):
        k = (j * 13) % nv
        oz, oy, ox = k // (ny * nx), (k // nx) % ny, k % nx
        v = ((zh + oz) % 2) * (ny * nx) + ((y + sign * oy + ny) % ny) * nx + (x + sign * ox + nx) % nx
        return v, (zl + oz) % 2

    def tau_copy(j):
        v, _ = peer(j, -1)
        return pltpu.make_async_copy(
            tau.at[:, pl.ds(pl.multiple_of(v * EB, EB), EB), :], tbuf.at[j % SLOTS], tau_sem.at[j % SLOTS]
        )

    mine = pl.ds(pl.multiple_of(me * EB, EB), EB)
    my_cols = pl.ds(pl.multiple_of(me * cw, cw), cw)
    local = [
        pltpu.make_async_copy(w.at[:, mine, :], wbuf.at[0], loc_sem.at[0]),
        pltpu.make_async_copy(wov, wovb, loc_sem.at[1]),
        pltpu.make_async_copy(foo, foob, loc_sem.at[2]),
        pltpu.make_async_copy(fvv, fvvb, loc_sem.at[3]),
        pltpu.make_async_copy(r2.at[:, pl.ds(0, pairs)], winb, loc_sem.at[4]),
        pltpu.make_async_copy(r2.at[:, my_cols], r2s.at[mine, :], loc_sem.at[5]),
        pltpu.make_async_copy(wo.at[:, my_cols], wos.at[me], loc_sem.at[6]),
        pltpu.make_async_copy(r1, r1b, loc_sem.at[7]),
    ]

    barrier = pltpu.get_barrier_semaphore()

    def greet(j, _):
        v, zd = peer(j, 1)
        pl.semaphore_signal(barrier, inc=1, device_id=(root, v), device_id_type=MESH)

        @pl.when(zd != zl)
        def _():
            pl.semaphore_signal(barrier, inc=1, device_id=(zd * 2 + c, v), device_id_type=MESH)

        return 0

    lax.fori_loop(1, nv, greet, 0)
    for other in (sibling, partner):
        pl.semaphore_signal(barrier, inc=1, device_id=other, device_id_type=MESH)
    for copy in local:
        copy.start()
    pl.semaphore_wait(barrier, nv - 1 + nv // 2 + 2)

    def small_copies(v):
        cols = pl.ds(pl.multiple_of(v * cw, cw), cw)
        return (
            pltpu.make_async_remote_copy(
                src_ref=r2.at[:, cols], dst_ref=r2s.at[mine, :], send_sem=small_send.at[0], recv_sem=small_recv.at[0],
                device_id=(root, v), device_id_type=MESH,
            ),
            pltpu.make_async_remote_copy(
                src_ref=wo.at[:, cols], dst_ref=wos.at[me], send_sem=small_send.at[1], recv_sem=small_recv.at[1],
                device_id=(root, v), device_id_type=MESH,
            ),
        )

    def send(j, _):
        v, zd = peer(j, 1)
        first = HALF * c + SHARE * zd
        pltpu.make_async_remote_copy(
            src_ref=w.at[pl.ds(first, LONG), pl.ds(pl.multiple_of(v * EB, EB), EB), :],
            dst_ref=wbuf.at[j, pl.ds(first, LONG)],
            send_sem=long_send.at[0],
            recv_sem=long_recv.at[j],
            device_id=(zd * 2 + c, v),
            device_id_type=MESH,
        ).start()
        for copy in small_copies(v):
            copy.start()
        return 0

    lax.fori_loop(1, nv, send, 0)

    i, j = iotas(EB * EB, EB * EB)
    perm[...] = onehot(((i >> 4) == (j & 15)) & ((i & 15) == (j >> 4)))

    local[3].wait()
    local[4].wait()
    i, j = iotas(EB, virt)
    chosen = dot(onehot(j == i + me * EB), fvvb[...], 1, 1).astype(BF16)
    acc[...] = dot(winb[...], chosen, 0, 0).reshape(acc.shape)

    def z_copy(j):
        part = wbuf.at[j, pl.ds(HALF * c + LONG * zl, SHARE)]
        return pltpu.make_async_remote_copy(
            src_ref=part, dst_ref=part, send_sem=z_send.at[0], recv_sem=z_recv.at[j], device_id=partner, device_id_type=MESH
        )

    def sib_copy(j):
        part = wbuf.at[j, pl.ds(HALF * c, HALF)]
        return pltpu.make_async_remote_copy(
            src_ref=part, dst_ref=part, send_sem=sib_send.at[0], recv_sem=sib_recv.at[j], device_id=sibling, device_id_type=MESH
        )

    def received(ref, sem):
        pltpu.make_async_copy(ref, ref, sem).wait()

    def compute(j):
        tau_copy(j).wait()
        block = tbuf[j % SLOTS].reshape(EB * EB, pairs)
        turned = dot(perm[...], block, 1, 0).astype(BF16)
        weights = wbuf[j].reshape(EB * EB, virt)
        step = pairs // 2
        for part in range(2):
            at = slice(part * step, (part + 1) * step)
            acc[part] += dot(turned[:, at], weights, 0, 0).reshape(acc.shape[1:])

    def advance(j, _):
        k, t = j - Z_LAG, j - LAG

        @pl.when(j < nv)
        def _():
            tau_copy(j).start()

        @pl.when((j >= 1) & (j < nv))
        def _():
            received(wbuf.at[j, pl.ds(HALF * c + SHARE * zl, LONG)], long_recv.at[j])
            z_copy(j).start()

        @pl.when((k >= 1) & (k < nv))
        def _():
            received(wbuf.at[k, pl.ds(HALF * c + LONG * (1 - zl), SHARE)], z_recv.at[k])
            sib_copy(k).start()

        @pl.when(t > 0)
        def _():
            received(wbuf.at[t, pl.ds(HALF * (1 - c), HALF)], sib_recv.at[t])

        @pl.when(t >= 0)
        def _():
            compute(lax.max(t, 0))

        return 0

    local[0].wait()
    middle = nv // 2
    lax.fori_loop(0, middle, advance, 0)

    local[1].wait()
    local[7].wait()
    i, j = iotas(nocc, nocc)
    spread = jnp.where(i == j, jnp.broadcast_to(r1b[...].astype(F32), (nocc, nocc)), 0.0).astype(BF16)
    winb32 = dot(spread, jnp.ones((nocc, 128), BF16), 1, 0)
    sing[...] = jnp.zeros_like(sing)
    for k in range(nocc):
        factor = jnp.broadcast_to(winb32[k : k + 1, 0:1], (rows, virt))
        sing[...] += factor * wovb[k].astype(F32)

    local[2].wait()
    local[5].wait()
    local[6].wait()
    others = (nv - 1) * EB
    received(r2s.at[pl.ds(0, others), :], small_recv.at[0])
    received(wos.at[pl.ds(0, nv - 1)], small_recv.at[1])
    held = r2s[...]
    fock = foob[...]
    m_first = me * (cw // nocc)
    i, j = iotas(nocc, cw)
    by_i = dot(fock, onehot(i == (j >> ob) + m_first), 0, 0).astype(BF16)
    by_j = dot(fock, onehot(i == (j & (nocc - 1))), 0, 0).astype(BF16)
    p, q = iotas(pairs, nocc)
    take_i = dot(onehot((p >> ob) == q), by_i, 1, 0)
    take_j = dot(onehot((p & (nocc - 1)) == q), by_j, 1, 0)
    p, q = iotas(pairs, cw)
    first = jnp.where((p & (nocc - 1)) == (q & (nocc - 1)), take_i, 0.0).astype(BF16)
    second = jnp.where((p >> ob) == (q >> ob) + m_first, take_j, 0.0).astype(BF16)
    quartic = wos[...].astype(F32).reshape(pairs, cw).astype(BF16)
    other_terms = dot(quartic, held, 1, 1) - dot(first, held, 1, 1) - dot(second, held, 1, 1)
    acc[...] += other_terms.reshape(acc.shape)

    lax.fori_loop(middle, nv + LAG, advance, 0)

    half = virt // 2
    left, right = pl.ds(0, half), pl.ds(half, half)

    def flat(z_at, y_at, x_at):
        return z_at * (ny * nx) + y_at * nx + x_at

    def along_x(ox):
        at = (x + ox) % nx
        return pltpu.make_async_remote_copy(
            src_ref=acc.at[:, :, at, :, left], dst_ref=first_x.at[ox - 1], send_sem=rs_send.at[0], recv_sem=rs_recv.at[0],
            device_id=(root, flat(zh, y, at)), device_id_type=MESH,
        )

    def along_y(oy):
        at = (y + oy) % ny
        return pltpu.make_async_remote_copy(
            src_ref=acc.at[:, at, :, :, right], dst_ref=first_y.at[oy - 1], send_sem=rs_send.at[1], recv_sem=rs_recv.at[1],
            device_id=(root, flat(zh, at, x)), device_id_type=MESH,
        )

    for offset in range(1, max(nx, ny)):
        if offset < nx:
            along_x(offset).start()
        if offset < ny:
            along_y(offset).start()

    received(first_x, rs_recv.at[0])
    total_x[...] = acc[:, :, x, :, :half] + jnp.sum(first_x[...], axis=0)

    def to_owner_x(q, _):
        z_at, y_at = (zh + q // ny) % 2, (y + q % ny) % ny
        pltpu.make_async_remote_copy(
            src_ref=total_x.at[z_at, y_at], dst_ref=last_x.at[q - 1], send_sem=rs_send.at[2], recv_sem=rs_recv.at[2],
            device_id=(root, flat(z_at, y_at, x)), device_id_type=MESH,
        ).start()
        return 0

    lax.fori_loop(1, 2 * ny, to_owner_x, 0)
    received(first_y, rs_recv.at[1])
    total_y[...] = acc[:, y, :, :, half:] + jnp.sum(first_y[...], axis=0)

    def to_owner_y(q, _):
        z_at, x_at = (zh + q // nx) % 2, (x + q % nx) % nx
        pltpu.make_async_remote_copy(
            src_ref=total_y.at[z_at, x_at], dst_ref=last_y.at[q - 1], send_sem=rs_send.at[3], recv_sem=rs_recv.at[3],
            device_id=(root, flat(z_at, y, x_at)), device_id_type=MESH,
        ).start()
        return 0

    lax.fori_loop(1, 2 * nx, to_owner_y, 0)
    received(wbuf.at[pl.ds(0, nv - 1), pl.ds(0, LONG)], long_send.at[0])
    received(wbuf.at[pl.ds(0, nv - 1), pl.ds(0, SHARE)], z_send.at[0])
    received(wbuf.at[pl.ds(0, nv - 1), pl.ds(0, HALF)], sib_send.at[0])
    received(r2s.at[pl.ds(0, others), :], small_send.at[0])
    received(wos.at[pl.ds(0, nv - 1)], small_send.at[1])
    received(first_x, rs_send.at[0])
    received(first_y, rs_send.at[1])
    received(last_x, rs_recv.at[2])
    out[:, :half] = total_x[zh, y] - sing[:, :half] + jnp.sum(last_x[...], axis=0)
    received(last_y, rs_recv.at[3])
    out[:, half:] = total_y[zh, x] - sing[:, half:] + jnp.sum(last_y[...], axis=0)
    received(last_x, rs_send.at[2])
    received(last_y, rs_send.at[3])


def on_device(r2, tau, w, wo, wov, foo, fvv, r1):
    nv = w.shape[1] // w.shape[0]
    side = int(math.isqrt(nv // 2))
    rows, virt, pairs, nocc = wo.shape[0], w.shape[2], tau.shape[2], foo.shape[0]
    cw, half = wo.shape[1] // nv, virt // 2
    dma = pltpu.SemaphoreType.DMA
    flops = 2 * nv * EB * EB * pairs * (virt + EB * EB)
    return pl.pallas_call(
        functools.partial(kernel, side, side),
        out_shape=jax.ShapeDtypeStruct((rows, virt), F32),
        in_specs=[pl.BlockSpec(memory_space=pl.ANY)] * 8,
        out_specs=pl.BlockSpec(memory_space=pltpu.VMEM),
        scratch_shapes=[
            pltpu.VMEM((nv, EB, EB, virt), BF16),
            pltpu.VMEM((SLOTS, EB, EB, pairs), BF16),
            pltpu.VMEM((2, side, side, rows, virt), F32),
            pltpu.VMEM((side - 1, 2, side, rows, half), F32),
            pltpu.VMEM((side - 1, 2, side, rows, half), F32),
            pltpu.VMEM((2, side, rows, half), F32),
            pltpu.VMEM((2, side, rows, half), F32),
            pltpu.VMEM((2 * side - 1, rows, half), F32),
            pltpu.VMEM((2 * side - 1, rows, half), F32),
            pltpu.VMEM((nocc, rows, virt), BF16),
            pltpu.VMEM((virt, cw), BF16),
            pltpu.VMEM((nv, rows, cw), BF16),
            pltpu.VMEM((nocc, nocc), BF16),
            pltpu.VMEM((virt, virt), BF16),
            pltpu.VMEM((EB, pairs), BF16),
            pltpu.VMEM((1, nocc), BF16),
            pltpu.VMEM((rows, virt), F32),
            pltpu.VMEM((EB * EB, EB * EB), BF16),
            dma((SLOTS,)), dma((8,)),
            dma((1,)), dma((nv,)), dma((1,)), dma((nv,)), dma((1,)), dma((nv,)),
            dma((2,)), dma((2,)), dma((4,)), dma((4,)),
        ],
        compiler_params=pltpu.CompilerParams(collective_id=0, has_side_effects=True, vmem_limit_bytes=56 * 2**20),
        cost_estimate=pl.CostEstimate(flops=flops, bytes_accessed=26_000_000, transcendentals=0),
        name="ladder",
    )(r2, tau, w, wo, wov, foo, fvv, r1.reshape(1, -1))


def solution(mesh):
    in_specs = (
        P("virt", "root"),
        P("virt", None, "root"),
        P("virt", None, None),
        P("virt", None),
        P(None, "virt", None),
        P(),
        P(),
        P("root"),
    )
    return jax.shard_map(
        on_device, mesh=mesh, in_specs=in_specs, out_specs=P(("root", "virt"), None), check_vma=False
    )
```

```python
import functools
import math

import jax
import jax.numpy as jnp
from jax import lax
from jax.experimental import pallas as pl
from jax.experimental.pallas import tpu as pltpu
from jax.sharding import PartitionSpec as P

MESH = pl.DeviceIdType.MESH
F32, BF16 = jnp.float32, jnp.bfloat16
EB = 16
HALF = 8
LONG = 5
SHARE = 3
SLOTS = 8
AHEAD = 5
Z_LAG = 5
S_LAG = 3
LAG = Z_LAG + S_LAG


def dot(a, b, ca, cb):
    return lax.dot_general(a, b, (((ca,), (cb,)), ((), ())), preferred_element_type=F32)


def iotas(rows, cols):
    return (lax.broadcasted_iota(jnp.int32, (rows, cols), 0), lax.broadcasted_iota(jnp.int32, (rows, cols), 1))


def onehot(mask):
    return jnp.where(mask, 1.0, 0.0).astype(BF16)


def kernel(
    ny, nx,
    r2, tau, w, wo, wov, foo, fvv, r1,
    out,
    wbuf, tbuf, acc, first_x, first_y, total_x, total_y, last_x, last_y, turned, cmat, wovb, r2s, wos, foob, fvvb, winb, r1b, sing, perm,
    tau_sem, loc_sem, long_send, long_recv, z_send, z_recv, sib_send, sib_recv, small_send, small_recv, rs_send, rs_recv,
):
    nv = 2 * ny * nx
    nocc = foo.shape[0]
    pairs = tau.shape[2]
    rows = pairs // nv
    cw = wo.shape[1] // nv
    virt = fvv.shape[0]
    ob = int(math.log2(nocc))
    root, me = lax.axis_index("root"), lax.axis_index("virt")
    zl, c = root // 2, root % 2
    zh, y, x = me // (ny * nx), (me // nx) % ny, me % nx
    sibling = (zl * 2 + 1 - c, me)
    partner = ((1 - zl) * 2 + c, me)

    def peer(j, sign):
        k = (j * 13) % nv
        oz, oy, ox = k // (ny * nx), (k // nx) % ny, k % nx
        v = ((zh + oz) % 2) * (ny * nx) + ((y + sign * oy + ny) % ny) * nx + (x + sign * ox + nx) % nx
        return v, (zl + oz) % 2

    def tau_copy(j):
        v, _ = peer(j, -1)
        return pltpu.make_async_copy(
            tau.at[:, pl.ds(pl.multiple_of(v * EB, EB), EB), :], tbuf.at[j % SLOTS], tau_sem.at[j % SLOTS]
        )

    mine = pl.ds(pl.multiple_of(me * EB, EB), EB)
    my_cols = pl.ds(pl.multiple_of(me * cw, cw), cw)
    local = [
        pltpu.make_async_copy(w.at[:, mine, :], wbuf.at[0], loc_sem.at[0]),
        pltpu.make_async_copy(wov, wovb, loc_sem.at[1]),
        pltpu.make_async_copy(foo, foob, loc_sem.at[2]),
        pltpu.make_async_copy(fvv, fvvb, loc_sem.at[3]),
        pltpu.make_async_copy(r2.at[:, pl.ds(0, pairs)], winb, loc_sem.at[4]),
        pltpu.make_async_copy(r2.at[:, my_cols], r2s.at[mine, :], loc_sem.at[5]),
        pltpu.make_async_copy(wo.at[:, my_cols], wos.at[me], loc_sem.at[6]),
        pltpu.make_async_copy(r1, r1b, loc_sem.at[7]),
    ]

    barrier = pltpu.get_barrier_semaphore()

    def greet(j, _):
        v, zd = peer(j, 1)
        pl.semaphore_signal(barrier, inc=1, device_id=(root, v), device_id_type=MESH)

        @pl.when(zd != zl)
        def _():
            pl.semaphore_signal(barrier, inc=1, device_id=(zd * 2 + c, v), device_id_type=MESH)

        return 0

    lax.fori_loop(1, nv, greet, 0)
    for other in (sibling, partner):
        pl.semaphore_signal(barrier, inc=1, device_id=other, device_id_type=MESH)
    for j in range(SLOTS):
        tau_copy(j).start()
    for copy in local:
        copy.start()
    pl.semaphore_wait(barrier, nv - 1 + nv // 2 + 2)

    def small_copies(v):
        cols = pl.ds(pl.multiple_of(v * cw, cw), cw)
        return (
            pltpu.make_async_remote_copy(
                src_ref=r2.at[:, cols], dst_ref=r2s.at[mine, :], send_sem=small_send.at[0], recv_sem=small_recv.at[0],
                device_id=(root, v), device_id_type=MESH,
            ),
            pltpu.make_async_remote_copy(
                src_ref=wo.at[:, cols], dst_ref=wos.at[me], send_sem=small_send.at[1], recv_sem=small_recv.at[1],
                device_id=(root, v), device_id_type=MESH,
            ),
        )

    def send(j, _):
        v, zd = peer(j, 1)
        first = HALF * c + SHARE * zd
        pltpu.make_async_remote_copy(
            src_ref=w.at[pl.ds(first, LONG), pl.ds(pl.multiple_of(v * EB, EB), EB), :],
            dst_ref=wbuf.at[j, pl.ds(first, LONG)],
            send_sem=long_send.at[0],
            recv_sem=long_recv.at[j],
            device_id=(zd * 2 + c, v),
            device_id_type=MESH,
        ).start()
        return 0

    def send_small(j, _):
        v, _zd = peer(j, 1)
        for copy in small_copies(v):
            copy.start()
        return 0

    lax.fori_loop(1, nv, send, 0)
    lax.fori_loop(1, nv, send_small, 0)

    i, j = iotas(EB * EB, EB * EB)
    perm[...] = onehot(((i >> 4) == (j & 15)) & ((i & 15) == (j >> 4)))

    local[3].wait()
    local[4].wait()
    i, j = iotas(EB, virt)
    chosen = dot(onehot(j == i + me * EB), fvvb[...], 1, 1).astype(BF16)
    acc[...] = dot(winb[...], chosen, 0, 0).reshape(acc.shape)

    def z_copy(j):
        part = wbuf.at[j, pl.ds(HALF * c + LONG * zl, SHARE)]
        return pltpu.make_async_remote_copy(
            src_ref=part, dst_ref=part, send_sem=z_send.at[0], recv_sem=z_recv.at[j], device_id=partner, device_id_type=MESH
        )

    def sib_copy(j):
        part = wbuf.at[j, pl.ds(HALF * c, HALF)]
        return pltpu.make_async_remote_copy(
            src_ref=part, dst_ref=part, send_sem=sib_send.at[0], recv_sem=sib_recv.at[j], device_id=sibling, device_id_type=MESH
        )

    def received(ref, sem):
        pltpu.make_async_copy(ref, ref, sem).wait()

    def prepare(j):
        tau_copy(j).wait()
        block = tbuf[j % SLOTS].reshape(EB * EB, pairs)
        turned[j] = dot(block, perm[...], 0, 0).astype(BF16)

        @pl.when(j + SLOTS < nv)
        def _():
            tau_copy(j + SLOTS).start()

    def compute(j):
        weights = wbuf[j].reshape(EB * EB, virt)
        step = pairs // 2
        for part in range(2):
            acc[part] += dot(turned[j, pl.ds(part * step, step)], weights, 1, 0).reshape(acc.shape[1:])

    def advance(j, _):
        k, t = j - Z_LAG, j - LAG

        @pl.when((j >= 1) & (j < nv))
        def _():
            received(wbuf.at[j, pl.ds(HALF * c + SHARE * zl, LONG)], long_recv.at[j])
            z_copy(j).start()

        @pl.when((k >= 1) & (k < nv))
        def _():
            received(wbuf.at[k, pl.ds(HALF * c + LONG * (1 - zl), SHARE)], z_recv.at[k])
            sib_copy(k).start()

        @pl.when(t > 0)
        def _():
            received(wbuf.at[t, pl.ds(HALF * (1 - c), HALF)], sib_recv.at[t])

        @pl.when(t >= 0)
        def _():
            compute(lax.max(t, 0))

        @pl.when(j + AHEAD < nv)
        def _():
            prepare(j + AHEAD)

        return 0

    def prepare_early(j, _):
        prepare(j)
        return 0

    lax.fori_loop(0, AHEAD, prepare_early, 0)
    local[0].wait()
    middle = nv // 2
    lax.fori_loop(0, middle, advance, 0)

    local[1].wait()
    local[7].wait()
    i, j = iotas(nocc, nocc)
    spread = jnp.where(i == j, jnp.broadcast_to(r1b[...].astype(F32), (nocc, nocc)), 0.0).astype(BF16)
    winb32 = dot(spread, jnp.ones((nocc, 128), BF16), 1, 0)
    sing[...] = jnp.zeros_like(sing)
    for k in range(nocc):
        factor = jnp.broadcast_to(winb32[k : k + 1, 0:1], (rows, virt))
        sing[...] += factor * wovb[k].astype(F32)

    local[2].wait()
    fock = foob[...]
    m_first = me * (cw // nocc)
    i, j = iotas(nocc, cw)
    by_i = dot(fock, onehot(i == (j >> ob) + m_first), 0, 0).astype(BF16)
    by_j = dot(fock, onehot(i == (j & (nocc - 1))), 0, 0).astype(BF16)
    p, q = iotas(pairs, nocc)
    take_i = dot(onehot((p >> ob) == q), by_i, 1, 0)
    take_j = dot(onehot((p & (nocc - 1)) == q), by_j, 1, 0)
    p, q = iotas(pairs, cw)
    cmat[0] = jnp.where((p & (nocc - 1)) == (q & (nocc - 1)), take_i, 0.0).astype(BF16)
    cmat[1] = jnp.where((p >> ob) == (q >> ob) + m_first, take_j, 0.0).astype(BF16)

    lax.fori_loop(middle, nv, advance, 0)

    local[5].wait()
    local[6].wait()
    others = (nv - 1) * EB
    received(r2s.at[pl.ds(0, others), :], small_recv.at[0])
    received(wos.at[pl.ds(0, nv - 1)], small_recv.at[1])
    held = r2s[...]
    quartic = wos[...].astype(F32).reshape(pairs, cw).astype(BF16)
    other_terms = dot(quartic, held, 1, 1) - dot(cmat[0], held, 1, 1) - dot(cmat[1], held, 1, 1)
    acc[...] += other_terms.reshape(acc.shape)

    lax.fori_loop(nv, nv + LAG, advance, 0)

    half = virt // 2
    left, right = pl.ds(0, half), pl.ds(half, half)

    def flat(z_at, y_at, x_at):
        return z_at * (ny * nx) + y_at * nx + x_at

    def along_x(ox):
        at = (x + ox) % nx
        return pltpu.make_async_remote_copy(
            src_ref=acc.at[:, :, at, :, left], dst_ref=first_x.at[ox - 1], send_sem=rs_send.at[0], recv_sem=rs_recv.at[0],
            device_id=(root, flat(zh, y, at)), device_id_type=MESH,
        )

    def along_y(oy):
        at = (y + oy) % ny
        return pltpu.make_async_remote_copy(
            src_ref=acc.at[:, at, :, :, right], dst_ref=first_y.at[oy - 1], send_sem=rs_send.at[1], recv_sem=rs_recv.at[1],
            device_id=(root, flat(zh, at, x)), device_id_type=MESH,
        )

    for offset in range(1, max(nx, ny)):
        if offset < nx:
            along_x(offset).start()
        if offset < ny:
            along_y(offset).start()

    received(first_x, rs_recv.at[0])
    total_x[...] = acc[:, :, x, :, :half] + jnp.sum(first_x[...], axis=0)

    def to_owner_x(q, _):
        z_at, y_at = (zh + q // ny) % 2, (y + q % ny) % ny
        pltpu.make_async_remote_copy(
            src_ref=total_x.at[z_at, y_at], dst_ref=last_x.at[q - 1], send_sem=rs_send.at[2], recv_sem=rs_recv.at[2],
            device_id=(root, flat(z_at, y_at, x)), device_id_type=MESH,
        ).start()
        return 0

    lax.fori_loop(1, 2 * ny, to_owner_x, 0)
    received(first_y, rs_recv.at[1])
    total_y[...] = acc[:, y, :, :, half:] + jnp.sum(first_y[...], axis=0)

    def to_owner_y(q, _):
        z_at, x_at = (zh + q // nx) % 2, (x + q % nx) % nx
        pltpu.make_async_remote_copy(
            src_ref=total_y.at[z_at, x_at], dst_ref=last_y.at[q - 1], send_sem=rs_send.at[3], recv_sem=rs_recv.at[3],
            device_id=(root, flat(z_at, y, x_at)), device_id_type=MESH,
        ).start()
        return 0

    lax.fori_loop(1, 2 * nx, to_owner_y, 0)
    received(wbuf.at[pl.ds(0, nv - 1), pl.ds(0, LONG)], long_send.at[0])
    received(wbuf.at[pl.ds(0, nv - 1), pl.ds(0, SHARE)], z_send.at[0])
    received(wbuf.at[pl.ds(0, nv - 1), pl.ds(0, HALF)], sib_send.at[0])
    received(r2s.at[pl.ds(0, others), :], small_send.at[0])
    received(wos.at[pl.ds(0, nv - 1)], small_send.at[1])
    received(first_x, rs_send.at[0])
    received(first_y, rs_send.at[1])
    received(last_x, rs_recv.at[2])
    out[:, :half] = total_x[zh, y] - sing[:, :half] + jnp.sum(last_x[...], axis=0)
    received(last_y, rs_recv.at[3])
    out[:, half:] = total_y[zh, x] - sing[:, half:] + jnp.sum(last_y[...], axis=0)
    received(last_x, rs_send.at[2])
    received(last_y, rs_send.at[3])


def on_device(r2, tau, w, wo, wov, foo, fvv, r1):
    nv = w.shape[1] // w.shape[0]
    side = int(math.isqrt(nv // 2))
    rows, virt, pairs, nocc = wo.shape[0], w.shape[2], tau.shape[2], foo.shape[0]
    cw, half = wo.shape[1] // nv, virt // 2
    dma = pltpu.SemaphoreType.DMA
    flops = 2 * nv * EB * EB * pairs * (virt + EB * EB)
    return pl.pallas_call(
        functools.partial(kernel, side, side),
        out_shape=jax.ShapeDtypeStruct((rows, virt), F32),
        in_specs=[pl.BlockSpec(memory_space=pl.ANY)] * 8,
        out_specs=pl.BlockSpec(memory_space=pltpu.VMEM),
        scratch_shapes=[
            pltpu.VMEM((nv, EB, EB, virt), BF16),
            pltpu.VMEM((SLOTS, EB, EB, pairs), BF16),
            pltpu.VMEM((2, side, side, rows, virt), F32),
            pltpu.VMEM((side - 1, 2, side, rows, half), F32),
            pltpu.VMEM((side - 1, 2, side, rows, half), F32),
            pltpu.VMEM((2, side, rows, half), F32),
            pltpu.VMEM((2, side, rows, half), F32),
            pltpu.VMEM((2 * side - 1, rows, half), F32),
            pltpu.VMEM((2 * side - 1, rows, half), F32),
            pltpu.VMEM((nv, pairs, EB * EB), BF16),
            pltpu.VMEM((2, pairs, cw), BF16),
            pltpu.VMEM((nocc, rows, virt), BF16),
            pltpu.VMEM((virt, cw), BF16),
            pltpu.VMEM((nv, rows, cw), BF16),
            pltpu.VMEM((nocc, nocc), BF16),
            pltpu.VMEM((virt, virt), BF16),
            pltpu.VMEM((EB, pairs), BF16),
            pltpu.VMEM((1, nocc), BF16),
            pltpu.VMEM((rows, virt), F32),
            pltpu.VMEM((EB * EB, EB * EB), BF16),
            dma((SLOTS,)), dma((8,)),
            dma((1,)), dma((nv,)), dma((1,)), dma((nv,)), dma((1,)), dma((nv,)),
            dma((2,)), dma((2,)), dma((4,)), dma((4,)),
        ],
        compiler_params=pltpu.CompilerParams(collective_id=0, has_side_effects=True, vmem_limit_bytes=56 * 2**20),
        cost_estimate=pl.CostEstimate(flops=flops, bytes_accessed=26_000_000, transcendentals=0),
        name="ladder",
    )(r2, tau, w, wo, wov, foo, fvv, r1.reshape(1, -1))


def solution(mesh):
    in_specs = (
        P("virt", "root"),
        P("virt", None, "root"),
        P("virt", None, None),
        P("virt", None),
        P(None, "virt", None),
        P(),
        P(),
        P("root"),
    )
    return jax.shard_map(
        on_device, mesh=mesh, in_specs=in_specs, out_specs=P(("root", "virt"), None), check_vma=False
    )
```

```python
import functools
import math

import jax
import jax.numpy as jnp
from jax import lax
from jax.experimental import pallas as pl
from jax.experimental.pallas import tpu as pltpu
from jax.sharding import PartitionSpec as P

MESH = pl.DeviceIdType.MESH
F32, BF16 = jnp.float32, jnp.bfloat16
EB = 16
HALF = 8
LONG = 5
SHARE = 3
SLOTS = 8
CHUNKS = 4
AHEAD = 5
Z_LAG = 5
S_LAG = 3
LAG = Z_LAG + S_LAG


def dot(a, b, ca, cb):
    return lax.dot_general(a, b, (((ca,), (cb,)), ((), ())), preferred_element_type=F32)


def iotas(rows, cols):
    return (lax.broadcasted_iota(jnp.int32, (rows, cols), 0), lax.broadcasted_iota(jnp.int32, (rows, cols), 1))


def onehot(mask):
    return jnp.where(mask, 1.0, 0.0).astype(BF16)


def kernel(
    ny, nx,
    r2, tau, w, wo, wov, foo, fvv, r1,
    out,
    wbuf, tbuf, acc, near, total, far, turned, cmat, wovb, r2s, wos, foob, fvvb, winb, r1b, sing, perm,
    tau_sem, loc_sem, long_send, long_recv, z_send, z_recv, sib_send, sib_recv, small_send, small_recv, rs_send, rs_recv,
):
    nv = 2 * ny * nx
    nocc = foo.shape[0]
    pairs = tau.shape[2]
    rows = pairs // nv
    cw = wo.shape[1] // nv
    virt = fvv.shape[0]
    ob = int(math.log2(nocc))
    root, me = lax.axis_index("root"), lax.axis_index("virt")
    zl, c = root // 2, root % 2
    zh, y, x = me // (ny * nx), (me // nx) % ny, me % nx
    sibling = (zl * 2 + 1 - c, me)
    partner = ((1 - zl) * 2 + c, me)

    def peer(j, sign):
        k = (j * 11) % nv
        oz, oy, ox = k // (ny * nx), (k // nx) % ny, k % nx
        v = ((zh + oz) % 2) * (ny * nx) + ((y + sign * oy + ny) % ny) * nx + (x + sign * ox + nx) % nx
        return v, (zl + oz) % 2

    def tau_copy(j):
        v, _ = peer(j, -1)
        return pltpu.make_async_copy(
            tau.at[:, pl.ds(pl.multiple_of(v * EB, EB), EB), :], tbuf.at[j % SLOTS], tau_sem.at[j % SLOTS]
        )

    mine = pl.ds(pl.multiple_of(me * EB, EB), EB)
    my_cols = pl.ds(pl.multiple_of(me * cw, cw), cw)
    local = [
        pltpu.make_async_copy(w.at[:, mine, :], wbuf.at[0], loc_sem.at[0]),
        pltpu.make_async_copy(wov, wovb, loc_sem.at[1]),
        pltpu.make_async_copy(foo, foob, loc_sem.at[2]),
        pltpu.make_async_copy(fvv, fvvb, loc_sem.at[3]),
        pltpu.make_async_copy(r2.at[:, pl.ds(0, pairs)], winb, loc_sem.at[4]),
        pltpu.make_async_copy(r2.at[:, my_cols], r2s.at[mine, :], loc_sem.at[5]),
        pltpu.make_async_copy(wo.at[:, my_cols], wos.at[me], loc_sem.at[6]),
        pltpu.make_async_copy(r1, r1b, loc_sem.at[7]),
    ]

    barrier = pltpu.get_barrier_semaphore()

    def greet(j, _):
        v, zd = peer(j, 1)
        pl.semaphore_signal(barrier, inc=1, device_id=(root, v), device_id_type=MESH)

        @pl.when(zd != zl)
        def _():
            pl.semaphore_signal(barrier, inc=1, device_id=(zd * 2 + c, v), device_id_type=MESH)

        return 0

    lax.fori_loop(1, nv, greet, 0)
    for other in (sibling, partner):
        pl.semaphore_signal(barrier, inc=1, device_id=other, device_id_type=MESH)
    for j in range(SLOTS):
        tau_copy(j).start()
    for copy in local:
        copy.start()
    pl.semaphore_wait(barrier, nv - 1 + nv // 2 + 2)

    def small_copies(v):
        cols = pl.ds(pl.multiple_of(v * cw, cw), cw)
        return (
            pltpu.make_async_remote_copy(
                src_ref=r2.at[:, cols], dst_ref=r2s.at[mine, :], send_sem=small_send.at[0], recv_sem=small_recv.at[0],
                device_id=(root, v), device_id_type=MESH,
            ),
            pltpu.make_async_remote_copy(
                src_ref=wo.at[:, cols], dst_ref=wos.at[me], send_sem=small_send.at[1], recv_sem=small_recv.at[1],
                device_id=(root, v), device_id_type=MESH,
            ),
        )

    def send(j, _):
        v, zd = peer(j, 1)
        first = HALF * c + SHARE * zd
        pltpu.make_async_remote_copy(
            src_ref=w.at[pl.ds(first, LONG), pl.ds(pl.multiple_of(v * EB, EB), EB), :],
            dst_ref=wbuf.at[j, pl.ds(first, LONG)],
            send_sem=long_send.at[0],
            recv_sem=long_recv.at[j],
            device_id=(zd * 2 + c, v),
            device_id_type=MESH,
        ).start()
        return 0

    def send_small(j, _):
        v, _zd = peer(j, 1)
        for copy in small_copies(v):
            copy.start()
        return 0

    lax.fori_loop(1, nv, send, 0)
    lax.fori_loop(1, nv, send_small, 0)

    i, j = iotas(EB * EB, EB * EB)
    perm[...] = onehot(((i >> 4) == (j & 15)) & ((i & 15) == (j >> 4)))

    local[3].wait()
    local[4].wait()
    i, j = iotas(EB, virt)
    chosen = dot(onehot(j == i + me * EB), fvvb[...], 1, 1).astype(BF16)
    columns = virt // CHUNKS

    def add_terms(value, old):
        for q in range(CHUNKS):
            piece = value[:, q * columns : (q + 1) * columns].reshape(acc.shape[1:])
            acc[q] = acc[q] + piece if old else piece

    add_terms(dot(winb[...], chosen, 0, 0), False)

    def z_copy(j):
        part = wbuf.at[j, pl.ds(HALF * c + LONG * zl, SHARE)]
        return pltpu.make_async_remote_copy(
            src_ref=part, dst_ref=part, send_sem=z_send.at[0], recv_sem=z_recv.at[j], device_id=partner, device_id_type=MESH
        )

    def sib_copy(j):
        part = wbuf.at[j, pl.ds(HALF * c, HALF)]
        return pltpu.make_async_remote_copy(
            src_ref=part, dst_ref=part, send_sem=sib_send.at[0], recv_sem=sib_recv.at[j], device_id=sibling, device_id_type=MESH
        )

    def received(ref, sem):
        pltpu.make_async_copy(ref, ref, sem).wait()

    def prepare(j):
        tau_copy(j).wait()
        block = tbuf[j % SLOTS].reshape(EB * EB, pairs)
        turned[j] = dot(block, perm[...], 0, 0).astype(BF16)

        @pl.when(j + SLOTS < nv)
        def _():
            tau_copy(j + SLOTS).start()

    def compute(j):
        weights = wbuf[j].reshape(EB * EB, virt)
        step = pairs // 2
        for part in range(2):
            product = dot(turned[j, pl.ds(part * step, step)], weights, 1, 0)
            for q in range(CHUNKS):
                acc[q, part] += product[:, q * columns : (q + 1) * columns].reshape(acc.shape[2:])

    def advance(j, _):
        k, t = j - Z_LAG, j - LAG

        @pl.when((j >= 1) & (j < nv))
        def _():
            received(wbuf.at[j, pl.ds(HALF * c + SHARE * zl, LONG)], long_recv.at[j])
            z_copy(j).start()

        @pl.when((k >= 1) & (k < nv))
        def _():
            received(wbuf.at[k, pl.ds(HALF * c + LONG * (1 - zl), SHARE)], z_recv.at[k])
            sib_copy(k).start()

        @pl.when(t > 0)
        def _():
            received(wbuf.at[t, pl.ds(HALF * (1 - c), HALF)], sib_recv.at[t])

        @pl.when(t >= 0)
        def _():
            compute(lax.max(t, 0))

        @pl.when(j + AHEAD < nv)
        def _():
            prepare(j + AHEAD)

        return 0

    def prepare_early(j, _):
        prepare(j)
        return 0

    lax.fori_loop(0, AHEAD, prepare_early, 0)
    local[0].wait()
    middle = nv // 2
    lax.fori_loop(0, middle, advance, 0)

    local[1].wait()
    local[7].wait()
    i, j = iotas(nocc, nocc)
    spread = jnp.where(i == j, jnp.broadcast_to(r1b[...].astype(F32), (nocc, nocc)), 0.0).astype(BF16)
    winb32 = dot(spread, jnp.ones((nocc, 128), BF16), 1, 0)
    sing[...] = jnp.zeros_like(sing)
    for k in range(nocc):
        factor = jnp.broadcast_to(winb32[k : k + 1, 0:1], (rows, virt))
        sing[...] += factor * wovb[k].astype(F32)

    local[2].wait()
    fock = foob[...]
    m_first = me * (cw // nocc)
    i, j = iotas(nocc, cw)
    by_i = dot(fock, onehot(i == (j >> ob) + m_first), 0, 0).astype(BF16)
    by_j = dot(fock, onehot(i == (j & (nocc - 1))), 0, 0).astype(BF16)
    p, q = iotas(pairs, nocc)
    take_i = dot(onehot((p >> ob) == q), by_i, 1, 0)
    take_j = dot(onehot((p & (nocc - 1)) == q), by_j, 1, 0)
    p, q = iotas(pairs, cw)
    cmat[0] = jnp.where((p & (nocc - 1)) == (q & (nocc - 1)), take_i, 0.0).astype(BF16)
    cmat[1] = jnp.where((p >> ob) == (q >> ob) + m_first, take_j, 0.0).astype(BF16)

    lax.fori_loop(middle, nv, advance, 0)

    local[5].wait()
    local[6].wait()
    others = (nv - 1) * EB
    received(r2s.at[pl.ds(0, others), :], small_recv.at[0])
    received(wos.at[pl.ds(0, nv - 1)], small_recv.at[1])
    held = r2s[...]
    quartic = wos[...].astype(F32).reshape(pairs, cw).astype(BF16)
    add_terms(dot(quartic, held, 1, 1) - dot(cmat[0], held, 1, 1) - dot(cmat[1], held, 1, 1), True)

    lax.fori_loop(nv, nv + LAG, advance, 0)

    side = nx

    def flat(z_at, y_at, x_at):
        return z_at * (ny * nx) + y_at * nx + x_at

    def line(q, at):
        return acc.at[q, :, at] if q % 2 else acc.at[q, :, :, at]

    def here(q):
        return y if q % 2 else x

    def cross(q):
        return x if q % 2 else y

    for q in range(CHUNKS):
        for offset in range(1, side):
            at = (here(q) + offset) % side
            pltpu.make_async_remote_copy(
                src_ref=line(q, at), dst_ref=near.at[q, offset - 1], send_sem=rs_send.at[q], recv_sem=rs_recv.at[q],
                device_id=(root, flat(zh, at, x) if q % 2 else flat(zh, y, at)), device_id_type=MESH,
            ).start()

    for q in range(CHUNKS):
        received(near.at[q], rs_recv.at[q])
        total[q] = line(q, here(q))[...] + jnp.sum(near[q], axis=0)

        def to_owner(i, _, q=q):
            z_at, at = (zh + i // side) % 2, (cross(q) + i % side) % side
            pltpu.make_async_remote_copy(
                src_ref=total.at[q, z_at, at], dst_ref=far.at[q, i - 1],
                send_sem=rs_send.at[CHUNKS + q], recv_sem=rs_recv.at[CHUNKS + q],
                device_id=(root, flat(z_at, y, at) if q % 2 else flat(z_at, at, x)), device_id_type=MESH,
            ).start()
            return 0

        lax.fori_loop(1, 2 * side, to_owner, 0)

    received(wbuf.at[pl.ds(0, nv - 1), pl.ds(0, LONG)], long_send.at[0])
    received(wbuf.at[pl.ds(0, nv - 1), pl.ds(0, SHARE)], z_send.at[0])
    received(wbuf.at[pl.ds(0, nv - 1), pl.ds(0, HALF)], sib_send.at[0])
    received(r2s.at[pl.ds(0, others), :], small_send.at[0])
    received(wos.at[pl.ds(0, nv - 1)], small_send.at[1])
    for q in range(CHUNKS):
        cols = slice(q * columns, (q + 1) * columns)
        received(far.at[q], rs_recv.at[CHUNKS + q])
        out[:, cols] = total[q, zh, cross(q)] - sing[:, cols] + jnp.sum(far[q], axis=0)
    for q in range(CHUNKS):
        received(near.at[q], rs_send.at[q])
        received(far.at[q], rs_send.at[CHUNKS + q])


def on_device(r2, tau, w, wo, wov, foo, fvv, r1):
    nv = w.shape[1] // w.shape[0]
    side = int(math.isqrt(nv // 2))
    rows, virt, pairs, nocc = wo.shape[0], w.shape[2], tau.shape[2], foo.shape[0]
    cw, columns = wo.shape[1] // nv, virt // CHUNKS
    dma = pltpu.SemaphoreType.DMA
    flops = 2 * nv * EB * EB * pairs * (virt + EB * EB)
    return pl.pallas_call(
        functools.partial(kernel, side, side),
        out_shape=jax.ShapeDtypeStruct((rows, virt), F32),
        in_specs=[pl.BlockSpec(memory_space=pl.ANY)] * 8,
        out_specs=pl.BlockSpec(memory_space=pltpu.VMEM),
        scratch_shapes=[
            pltpu.VMEM((nv, EB, EB, virt), BF16),
            pltpu.VMEM((SLOTS, EB, EB, pairs), BF16),
            pltpu.VMEM((CHUNKS, 2, side, side, rows, columns), F32),
            pltpu.VMEM((CHUNKS, side - 1, 2, side, rows, columns), F32),
            pltpu.VMEM((CHUNKS, 2, side, rows, columns), F32),
            pltpu.VMEM((CHUNKS, 2 * side - 1, rows, columns), F32),
            pltpu.VMEM((nv, pairs, EB * EB), BF16),
            pltpu.VMEM((2, pairs, cw), BF16),
            pltpu.VMEM((nocc, rows, virt), BF16),
            pltpu.VMEM((virt, cw), BF16),
            pltpu.VMEM((nv, rows, cw), BF16),
            pltpu.VMEM((nocc, nocc), BF16),
            pltpu.VMEM((virt, virt), BF16),
            pltpu.VMEM((EB, pairs), BF16),
            pltpu.VMEM((1, nocc), BF16),
            pltpu.VMEM((rows, virt), F32),
            pltpu.VMEM((EB * EB, EB * EB), BF16),
            dma((SLOTS,)), dma((8,)),
            dma((1,)), dma((nv,)), dma((1,)), dma((nv,)), dma((1,)), dma((nv,)),
            dma((2,)), dma((2,)), dma((2 * CHUNKS,)), dma((2 * CHUNKS,)),
        ],
        compiler_params=pltpu.CompilerParams(collective_id=0, has_side_effects=True, vmem_limit_bytes=56 * 2**20),
        cost_estimate=pl.CostEstimate(flops=flops, bytes_accessed=26_000_000, transcendentals=0),
        name="ladder",
    )(r2, tau, w, wo, wov, foo, fvv, r1.reshape(1, -1))


def solution(mesh):
    in_specs = (
        P("virt", "root"),
        P("virt", None, "root"),
        P("virt", None, None),
        P("virt", None),
        P(None, "virt", None),
        P(),
        P(),
        P("root"),
    )
    return jax.shard_map(
        on_device, mesh=mesh, in_specs=in_specs, out_specs=P(("root", "virt"), None), check_vma=False
    )
```

```python
import functools
import math

import jax
import jax.numpy as jnp
from jax import lax
from jax.experimental import pallas as pl
from jax.experimental.pallas import tpu as pltpu
from jax.sharding import PartitionSpec as P

MESH = pl.DeviceIdType.MESH
F32, BF16 = jnp.float32, jnp.bfloat16
EB = 16
HALF = 8
LONG = 5
SHARE = 3
SLOTS = 8
UNDER = 12
CHUNKS = 4
AHEAD = 5
Z_LAG = 5
S_LAG = 3
LAG = Z_LAG + S_LAG


def dot(a, b, ca, cb):
    return lax.dot_general(a, b, (((ca,), (cb,)), ((), ())), preferred_element_type=F32)


def iotas(rows, cols):
    return (lax.broadcasted_iota(jnp.int32, (rows, cols), 0), lax.broadcasted_iota(jnp.int32, (rows, cols), 1))


def onehot(mask):
    return jnp.where(mask, 1.0, 0.0).astype(BF16)


def kernel(
    ny, nx,
    r2, tau, w, wo, wov, foo, fvv, r1,
    out,
    wbuf, tbuf, acc, near, total, far, turned, cmat, wovb, r2s, wos, foob, fvvb, winb, r1b, sing, perm,
    tau_sem, loc_sem, long_send, long_recv, z_send, z_recv, sib_send, sib_recv, small_send, small_recv, rs_send, rs_recv,
):
    nv = 2 * ny * nx
    rounds = nv - 1
    steps = 2 * rounds
    nocc = foo.shape[0]
    pairs = tau.shape[2]
    rows = pairs // nv
    cw = wo.shape[1] // nv
    virt = fvv.shape[0]
    half = virt // 2
    ob = int(math.log2(nocc))
    root, me = lax.axis_index("root"), lax.axis_index("virt")
    zl, c = root // 2, root % 2
    zh, y, x = me // (ny * nx), (me // nx) % ny, me % nx
    sibling = (zl * 2 + 1 - c, me)
    partner = ((1 - zl) * 2 + c, me)

    def peer(j, sign):
        k = (j * 11) % nv
        oz, oy, ox = k // (ny * nx), (k // nx) % ny, k % nx
        v = ((zh + oz) % 2) * (ny * nx) + ((y + sign * oy + ny) % ny) * nx + (x + sign * ox + nx) % nx
        return v, (zl + oz) % 2

    def tau_copy(j):
        v, _ = peer(j, -1)
        return pltpu.make_async_copy(
            tau.at[:, pl.ds(pl.multiple_of(v * EB, EB), EB), :], tbuf.at[j % SLOTS], tau_sem.at[j % SLOTS]
        )

    mine = pl.ds(pl.multiple_of(me * EB, EB), EB)
    my_cols = pl.ds(pl.multiple_of(me * cw, cw), cw)
    local = [
        pltpu.make_async_copy(w.at[:, mine, pl.ds(0, half)], wbuf.at[steps], loc_sem.at[0]),
        pltpu.make_async_copy(wov, wovb, loc_sem.at[1]),
        pltpu.make_async_copy(foo, foob, loc_sem.at[2]),
        pltpu.make_async_copy(fvv, fvvb, loc_sem.at[3]),
        pltpu.make_async_copy(r2.at[:, pl.ds(0, pairs)], winb, loc_sem.at[4]),
        pltpu.make_async_copy(r2.at[:, my_cols], r2s.at[mine, :], loc_sem.at[5]),
        pltpu.make_async_copy(wo.at[:, my_cols], wos.at[me], loc_sem.at[6]),
        pltpu.make_async_copy(r1, r1b, loc_sem.at[7]),
        pltpu.make_async_copy(w.at[:, mine, pl.ds(half, half)], wbuf.at[steps + 1], loc_sem.at[8]),
    ]

    barrier = pltpu.get_barrier_semaphore()

    def greet(j, _):
        v, zd = peer(j, 1)
        pl.semaphore_signal(barrier, inc=1, device_id=(root, v), device_id_type=MESH)

        @pl.when(zd != zl)
        def _():
            pl.semaphore_signal(barrier, inc=1, device_id=(zd * 2 + c, v), device_id_type=MESH)

        return 0

    lax.fori_loop(1, nv, greet, 0)
    for other in (sibling, partner):
        pl.semaphore_signal(barrier, inc=1, device_id=other, device_id_type=MESH)
    for j in range(SLOTS):
        tau_copy(j).start()
    for copy in local:
        copy.start()
    pl.semaphore_wait(barrier, nv - 1 + nv // 2 + 2)

    def small_copies(v):
        cols = pl.ds(pl.multiple_of(v * cw, cw), cw)
        return (
            pltpu.make_async_remote_copy(
                src_ref=r2.at[:, cols], dst_ref=r2s.at[mine, :], send_sem=small_send.at[0], recv_sem=small_recv.at[0],
                device_id=(root, v), device_id_type=MESH,
            ),
            pltpu.make_async_remote_copy(
                src_ref=wo.at[:, cols], dst_ref=wos.at[me], send_sem=small_send.at[1], recv_sem=small_recv.at[1],
                device_id=(root, v), device_id_type=MESH,
            ),
        )

    def send(step, _):
        v, zd = peer(step % rounds + 1, 1)
        first = HALF * c + SHARE * zd
        cols = pl.ds(pl.multiple_of((step // rounds) * half, half), half)
        pltpu.make_async_remote_copy(
            src_ref=w.at[pl.ds(first, LONG), pl.ds(pl.multiple_of(v * EB, EB), EB), cols],
            dst_ref=wbuf.at[step, pl.ds(first, LONG)],
            send_sem=long_send.at[0],
            recv_sem=long_recv.at[step],
            device_id=(zd * 2 + c, v),
            device_id_type=MESH,
        ).start()
        return 0

    def send_small(j, _):
        v, _zd = peer(j, 1)
        for copy in small_copies(v):
            copy.start()
        return 0

    lax.fori_loop(0, rounds, send, 0)
    lax.fori_loop(1, nv, send_small, 0)
    lax.fori_loop(rounds, steps, send, 0)

    i, j = iotas(EB * EB, EB * EB)
    perm[...] = onehot(((i >> 4) == (j & 15)) & ((i & 15) == (j >> 4)))

    local[3].wait()
    local[4].wait()
    i, j = iotas(EB, virt)
    chosen = dot(onehot(j == i + me * EB), fvvb[...], 1, 1).astype(BF16)
    columns = virt // CHUNKS

    def add_terms(value, old):
        for q in range(CHUNKS):
            piece = value[:, q * columns : (q + 1) * columns].reshape(acc.shape[1:])
            acc[q] = acc[q] + piece if old else piece

    add_terms(dot(winb[...], chosen, 0, 0), False)

    def z_copy(j):
        part = wbuf.at[j, pl.ds(HALF * c + LONG * zl, SHARE)]
        return pltpu.make_async_remote_copy(
            src_ref=part, dst_ref=part, send_sem=z_send.at[0], recv_sem=z_recv.at[j], device_id=partner, device_id_type=MESH
        )

    def sib_copy(j):
        part = wbuf.at[j, pl.ds(HALF * c, HALF)]
        return pltpu.make_async_remote_copy(
            src_ref=part, dst_ref=part, send_sem=sib_send.at[0], recv_sem=sib_recv.at[j], device_id=sibling, device_id_type=MESH
        )

    def received(ref, sem):
        pltpu.make_async_copy(ref, ref, sem).wait()

    def prepare(j):
        tau_copy(j).wait()
        block = tbuf[j % SLOTS].reshape(EB * EB, pairs)
        turned[j] = dot(block, perm[...], 0, 0).astype(BF16)

        @pl.when(j + SLOTS < nv)
        def _():
            tau_copy(j + SLOTS).start()

    def compute(j, slot, h):
        weights = wbuf[slot].reshape(EB * EB, half)
        size = pairs // 2
        for part in range(2):
            product = dot(turned[j, pl.ds(part * size, size)], weights, 1, 0)
            for q in range(CHUNKS // 2):
                acc[h * (CHUNKS // 2) + q, part] += product[:, q * columns : (q + 1) * columns].reshape(acc.shape[2:])

    def advance(i, _):
        k, t = i - Z_LAG, i - LAG

        @pl.when(i < steps)
        def _():
            received(wbuf.at[i, pl.ds(HALF * c + SHARE * zl, LONG)], long_recv.at[i])
            z_copy(i).start()

        @pl.when((k >= 0) & (k < steps))
        def _():
            received(wbuf.at[k, pl.ds(HALF * c + LONG * (1 - zl), SHARE)], z_recv.at[k])
            sib_copy(k).start()

        @pl.when(t >= 0)
        def _():
            at = lax.max(t, 0)
            received(wbuf.at[at, pl.ds(HALF * (1 - c), HALF)], sib_recv.at[at])
            compute(at % rounds + 1, at, at // rounds)

        @pl.when(i + AHEAD < nv)
        def _():
            prepare(i + AHEAD)

        return 0

    def prepare_early(j, _):
        prepare(j)
        return 0

    lax.fori_loop(0, AHEAD, prepare_early, 0)
    local[0].wait()
    local[8].wait()
    for h in range(2):
        compute(0, steps + h, h)
    middle = nv // 2
    lax.fori_loop(0, middle, advance, 0)

    local[1].wait()
    local[7].wait()
    i, j = iotas(nocc, nocc)
    spread = jnp.where(i == j, jnp.broadcast_to(r1b[...].astype(F32), (nocc, nocc)), 0.0).astype(BF16)
    winb32 = dot(spread, jnp.ones((nocc, 128), BF16), 1, 0)
    sing[...] = jnp.zeros_like(sing)
    for k in range(nocc):
        factor = jnp.broadcast_to(winb32[k : k + 1, 0:1], (rows, virt))
        sing[...] += factor * wovb[k].astype(F32)

    local[2].wait()
    fock = foob[...]
    m_first = me * (cw // nocc)
    i, j = iotas(nocc, cw)
    by_i = dot(fock, onehot(i == (j >> ob) + m_first), 0, 0).astype(BF16)
    by_j = dot(fock, onehot(i == (j & (nocc - 1))), 0, 0).astype(BF16)
    p, q = iotas(pairs, nocc)
    take_i = dot(onehot((p >> ob) == q), by_i, 1, 0)
    take_j = dot(onehot((p & (nocc - 1)) == q), by_j, 1, 0)
    p, q = iotas(pairs, cw)
    cmat[0] = jnp.where((p & (nocc - 1)) == (q & (nocc - 1)), take_i, 0.0).astype(BF16)
    cmat[1] = jnp.where((p >> ob) == (q >> ob) + m_first, take_j, 0.0).astype(BF16)

    lax.fori_loop(middle, rounds + LAG, advance, 0)

    local[5].wait()
    local[6].wait()
    others = (nv - 1) * EB
    received(r2s.at[pl.ds(0, others), :], small_recv.at[0])
    received(wos.at[pl.ds(0, nv - 1)], small_recv.at[1])
    held = r2s[...]
    quartic = wos[...].astype(F32).reshape(pairs, cw).astype(BF16)
    add_terms(dot(quartic, held, 1, 1) - dot(cmat[0], held, 1, 1) - dot(cmat[1], held, 1, 1), True)

    side = nx

    def flat(z_at, y_at, x_at):
        return z_at * (ny * nx) + y_at * nx + x_at

    def line(q, at):
        return acc.at[q, :, at] if q % 2 else acc.at[q, :, :, at]

    def here(q):
        return y if q % 2 else x

    def cross(q):
        return x if q % 2 else y

    def to_line(q):
        for offset in range(1, side):
            at = (here(q) + offset) % side
            pltpu.make_async_remote_copy(
                src_ref=line(q, at), dst_ref=near.at[q, offset - 1], send_sem=rs_send.at[q], recv_sem=rs_recv.at[q],
                device_id=(root, flat(zh, at, x) if q % 2 else flat(zh, y, at)), device_id_type=MESH,
            ).start()

    def to_owners(q):
        received(near.at[q], rs_recv.at[q])
        total[q] = line(q, here(q))[...] + jnp.sum(near[q], axis=0)

        def to_owner(i, _):
            z_at, at = (zh + i // side) % 2, (cross(q) + i % side) % side
            pltpu.make_async_remote_copy(
                src_ref=total.at[q, z_at, at], dst_ref=far.at[q, i - 1],
                send_sem=rs_send.at[CHUNKS + q], recv_sem=rs_recv.at[CHUNKS + q],
                device_id=(root, flat(z_at, y, at) if q % 2 else flat(z_at, at, x)), device_id_type=MESH,
            ).start()
            return 0

        lax.fori_loop(1, 2 * side, to_owner, 0)

    ready, over = rounds + LAG, steps + LAG
    for q in range(CHUNKS // 2):
        to_line(q)
    lax.fori_loop(ready, min(ready + UNDER, over), advance, 0)
    for q in range(CHUNKS // 2):
        to_owners(q)
    lax.fori_loop(min(ready + UNDER, over), over, advance, 0)
    for q in range(CHUNKS // 2, CHUNKS):
        to_line(q)
    for q in range(CHUNKS // 2, CHUNKS):
        to_owners(q)

    received(wbuf.at[pl.ds(0, steps), pl.ds(0, LONG)], long_send.at[0])
    received(wbuf.at[pl.ds(0, steps), pl.ds(0, SHARE)], z_send.at[0])
    received(wbuf.at[pl.ds(0, steps), pl.ds(0, HALF)], sib_send.at[0])
    received(r2s.at[pl.ds(0, others), :], small_send.at[0])
    received(wos.at[pl.ds(0, nv - 1)], small_send.at[1])
    for q in range(CHUNKS):
        cols = slice(q * columns, (q + 1) * columns)
        received(far.at[q], rs_recv.at[CHUNKS + q])
        out[:, cols] = total[q, zh, cross(q)] - sing[:, cols] + jnp.sum(far[q], axis=0)
    for q in range(CHUNKS):
        received(near.at[q], rs_send.at[q])
        received(far.at[q], rs_send.at[CHUNKS + q])


def on_device(r2, tau, w, wo, wov, foo, fvv, r1):
    nv = w.shape[1] // w.shape[0]
    side = int(math.isqrt(nv // 2))
    rows, virt, pairs, nocc = wo.shape[0], w.shape[2], tau.shape[2], foo.shape[0]
    cw, columns = wo.shape[1] // nv, virt // CHUNKS
    dma = pltpu.SemaphoreType.DMA
    flops = 2 * nv * EB * EB * pairs * (virt + EB * EB)
    return pl.pallas_call(
        functools.partial(kernel, side, side),
        out_shape=jax.ShapeDtypeStruct((rows, virt), F32),
        in_specs=[pl.BlockSpec(memory_space=pl.ANY)] * 8,
        out_specs=pl.BlockSpec(memory_space=pltpu.VMEM),
        scratch_shapes=[
            pltpu.VMEM((2 * nv, EB, EB, virt // 2), BF16),
            pltpu.VMEM((SLOTS, EB, EB, pairs), BF16),
            pltpu.VMEM((CHUNKS, 2, side, side, rows, columns), F32),
            pltpu.VMEM((CHUNKS, side - 1, 2, side, rows, columns), F32),
            pltpu.VMEM((CHUNKS, 2, side, rows, columns), F32),
            pltpu.VMEM((CHUNKS, 2 * side - 1, rows, columns), F32),
            pltpu.VMEM((nv, pairs, EB * EB), BF16),
            pltpu.VMEM((2, pairs, cw), BF16),
            pltpu.VMEM((nocc, rows, virt), BF16),
            pltpu.VMEM((virt, cw), BF16),
            pltpu.VMEM((nv, rows, cw), BF16),
            pltpu.VMEM((nocc, nocc), BF16),
            pltpu.VMEM((virt, virt), BF16),
            pltpu.VMEM((EB, pairs), BF16),
            pltpu.VMEM((1, nocc), BF16),
            pltpu.VMEM((rows, virt), F32),
            pltpu.VMEM((EB * EB, EB * EB), BF16),
            dma((SLOTS,)), dma((9,)),
            dma((1,)), dma((2 * nv,)), dma((1,)), dma((2 * nv,)), dma((1,)), dma((2 * nv,)),
            dma((2,)), dma((2,)), dma((2 * CHUNKS,)), dma((2 * CHUNKS,)),
        ],
        compiler_params=pltpu.CompilerParams(collective_id=0, has_side_effects=True, vmem_limit_bytes=56 * 2**20),
        cost_estimate=pl.CostEstimate(flops=flops, bytes_accessed=26_000_000, transcendentals=0),
        name="ladder",
    )(r2, tau, w, wo, wov, foo, fvv, r1.reshape(1, -1))


def solution(mesh):
    in_specs = (
        P("virt", "root"),
        P("virt", None, "root"),
        P("virt", None, None),
        P("virt", None),
        P(None, "virt", None),
        P(),
        P(),
        P("root"),
    )
    return jax.shard_map(
        on_device, mesh=mesh, in_specs=in_specs, out_specs=P(("root", "virt"), None), check_vma=False
    )
```

```python
import functools
import math

import jax
import jax.numpy as jnp
from jax import lax
from jax.experimental import pallas as pl
from jax.experimental.pallas import tpu as pltpu
from jax.sharding import PartitionSpec as P

MESH = pl.DeviceIdType.MESH
F32, BF16 = jnp.float32, jnp.bfloat16
EB = 16
HALF = 8
LONG = 5
SHARE = 3
SLOTS = 8
UNDER = 18
CHUNKS = 4
AHEAD = 5
Z_LAG = 12
S_LAG = 5
LAG = Z_LAG + S_LAG


def dot(a, b, ca, cb):
    return lax.dot_general(a, b, (((ca,), (cb,)), ((), ())), preferred_element_type=F32)


def iotas(rows, cols):
    return (lax.broadcasted_iota(jnp.int32, (rows, cols), 0), lax.broadcasted_iota(jnp.int32, (rows, cols), 1))


def onehot(mask):
    return jnp.where(mask, 1.0, 0.0).astype(BF16)


def kernel(
    ny, nx,
    r2, tau, w, wo, wov, foo, fvv, r1,
    out,
    wbuf, tbuf, acc, near, total, far, turned, cmat, wovb, r2s, wos, foob, fvvb, winb, r1b, sing, perm,
    tau_sem, loc_sem, long_send, long_recv, z_send, z_recv, sib_send, sib_recv, small_send, small_recv, rs_send, rs_recv,
):
    nv = 2 * ny * nx
    rounds = nv - 1
    steps = 2 * rounds
    nocc = foo.shape[0]
    pairs = tau.shape[2]
    rows = pairs // nv
    cw = wo.shape[1] // nv
    virt = fvv.shape[0]
    half = virt // 2
    ob = int(math.log2(nocc))
    root, me = lax.axis_index("root"), lax.axis_index("virt")
    zl, c = root // 2, root % 2
    zh, y, x = me // (ny * nx), (me // nx) % ny, me % nx
    sibling = (zl * 2 + 1 - c, me)
    partner = ((1 - zl) * 2 + c, me)

    def peer(j, sign):
        k = (j * 11) % nv
        oz, oy, ox = k // (ny * nx), (k // nx) % ny, k % nx
        v = ((zh + oz) % 2) * (ny * nx) + ((y + sign * oy + ny) % ny) * nx + (x + sign * ox + nx) % nx
        return v, (zl + oz) % 2

    def tau_copy(j):
        v, _ = peer(j, -1)
        return pltpu.make_async_copy(
            tau.at[:, pl.ds(pl.multiple_of(v * EB, EB), EB), :], tbuf.at[j % SLOTS], tau_sem.at[j % SLOTS]
        )

    mine = pl.ds(pl.multiple_of(me * EB, EB), EB)
    my_cols = pl.ds(pl.multiple_of(me * cw, cw), cw)
    local = [
        pltpu.make_async_copy(w.at[:, mine, pl.ds(0, half)], wbuf.at[steps], loc_sem.at[0]),
        pltpu.make_async_copy(wov, wovb, loc_sem.at[1]),
        pltpu.make_async_copy(foo, foob, loc_sem.at[2]),
        pltpu.make_async_copy(fvv, fvvb, loc_sem.at[3]),
        pltpu.make_async_copy(r2.at[:, pl.ds(0, pairs)], winb, loc_sem.at[4]),
        pltpu.make_async_copy(r2.at[:, my_cols], r2s.at[mine, :], loc_sem.at[5]),
        pltpu.make_async_copy(wo.at[:, my_cols], wos.at[me], loc_sem.at[6]),
        pltpu.make_async_copy(r1, r1b, loc_sem.at[7]),
        pltpu.make_async_copy(w.at[:, mine, pl.ds(half, half)], wbuf.at[steps + 1], loc_sem.at[8]),
    ]

    barrier = pltpu.get_barrier_semaphore()

    def greet(j, _):
        v, zd = peer(j, 1)
        pl.semaphore_signal(barrier, inc=1, device_id=(root, v), device_id_type=MESH)

        @pl.when(zd != zl)
        def _():
            pl.semaphore_signal(barrier, inc=1, device_id=(zd * 2 + c, v), device_id_type=MESH)

        return 0

    lax.fori_loop(1, nv, greet, 0)
    for other in (sibling, partner):
        pl.semaphore_signal(barrier, inc=1, device_id=other, device_id_type=MESH)
    for j in range(SLOTS):
        tau_copy(j).start()
    for copy in local:
        copy.start()
    pl.semaphore_wait(barrier, nv - 1 + nv // 2 + 2)

    def small_copies(v):
        cols = pl.ds(pl.multiple_of(v * cw, cw), cw)
        return (
            pltpu.make_async_remote_copy(
                src_ref=r2.at[:, cols], dst_ref=r2s.at[mine, :], send_sem=small_send.at[0], recv_sem=small_recv.at[0],
                device_id=(root, v), device_id_type=MESH,
            ),
            pltpu.make_async_remote_copy(
                src_ref=wo.at[:, cols], dst_ref=wos.at[me], send_sem=small_send.at[1], recv_sem=small_recv.at[1],
                device_id=(root, v), device_id_type=MESH,
            ),
        )

    def send(step, _):
        v, zd = peer(step % rounds + 1, 1)
        first = HALF * c + SHARE * zd
        cols = pl.ds(pl.multiple_of((step // rounds) * half, half), half)
        pltpu.make_async_remote_copy(
            src_ref=w.at[pl.ds(first, LONG), pl.ds(pl.multiple_of(v * EB, EB), EB), cols],
            dst_ref=wbuf.at[step, pl.ds(first, LONG)],
            send_sem=long_send.at[0],
            recv_sem=long_recv.at[step],
            device_id=(zd * 2 + c, v),
            device_id_type=MESH,
        ).start()
        return 0

    def send_small(j, _):
        v, _zd = peer(j, 1)
        for copy in small_copies(v):
            copy.start()
        return 0

    lax.fori_loop(0, rounds, send, 0)
    lax.fori_loop(1, nv, send_small, 0)
    lax.fori_loop(rounds, steps, send, 0)

    i, j = iotas(EB * EB, EB * EB)
    perm[...] = onehot(((i >> 4) == (j & 15)) & ((i & 15) == (j >> 4)))

    local[3].wait()
    local[4].wait()
    i, j = iotas(EB, virt)
    chosen = dot(onehot(j == i + me * EB), fvvb[...], 1, 1).astype(BF16)
    columns = virt // CHUNKS

    def add_terms(value, old):
        for q in range(CHUNKS):
            piece = value[:, q * columns : (q + 1) * columns].reshape(acc.shape[1:])
            acc[q] = acc[q] + piece if old else piece

    add_terms(dot(winb[...], chosen, 0, 0), False)

    def z_copy(j):
        part = wbuf.at[j, pl.ds(HALF * c + LONG * zl, SHARE)]
        return pltpu.make_async_remote_copy(
            src_ref=part, dst_ref=part, send_sem=z_send.at[0], recv_sem=z_recv.at[j], device_id=partner, device_id_type=MESH
        )

    def sib_copy(j):
        part = wbuf.at[j, pl.ds(HALF * c, HALF)]
        return pltpu.make_async_remote_copy(
            src_ref=part, dst_ref=part, send_sem=sib_send.at[0], recv_sem=sib_recv.at[j], device_id=sibling, device_id_type=MESH
        )

    def received(ref, sem):
        pltpu.make_async_copy(ref, ref, sem).wait()

    def prepare(j):
        tau_copy(j).wait()
        block = tbuf[j % SLOTS].reshape(EB * EB, pairs)
        turned[j] = dot(block, perm[...], 0, 0).astype(BF16)

        @pl.when(j + SLOTS < nv)
        def _():
            tau_copy(j + SLOTS).start()

    def compute(j, slot, h):
        weights = wbuf[slot].reshape(EB * EB, half)
        size = pairs // 2
        for part in range(2):
            product = dot(turned[j, pl.ds(part * size, size)], weights, 1, 0)
            for q in range(CHUNKS // 2):
                acc[h * (CHUNKS // 2) + q, part] += product[:, q * columns : (q + 1) * columns].reshape(acc.shape[2:])

    def advance(i, _):
        k, t = i - Z_LAG, i - LAG

        @pl.when(i < steps)
        def _():
            received(wbuf.at[i, pl.ds(HALF * c + SHARE * zl, LONG)], long_recv.at[i])
            z_copy(i).start()

        @pl.when((k >= 0) & (k < steps))
        def _():
            received(wbuf.at[k, pl.ds(HALF * c + LONG * (1 - zl), SHARE)], z_recv.at[k])
            sib_copy(k).start()

        @pl.when(t >= 0)
        def _():
            at = lax.max(t, 0)
            received(wbuf.at[at, pl.ds(HALF * (1 - c), HALF)], sib_recv.at[at])
            compute(at % rounds + 1, at, at // rounds)

        @pl.when(i + AHEAD < nv)
        def _():
            prepare(i + AHEAD)

        return 0

    def prepare_early(j, _):
        prepare(j)
        return 0

    lax.fori_loop(0, AHEAD, prepare_early, 0)
    local[0].wait()
    local[8].wait()
    for h in range(2):
        compute(0, steps + h, h)
    middle = nv // 2
    lax.fori_loop(0, middle, advance, 0)

    local[1].wait()
    local[7].wait()
    i, j = iotas(nocc, nocc)
    spread = jnp.where(i == j, jnp.broadcast_to(r1b[...].astype(F32), (nocc, nocc)), 0.0).astype(BF16)
    winb32 = dot(spread, jnp.ones((nocc, 128), BF16), 1, 0)
    sing[...] = jnp.zeros_like(sing)
    for k in range(nocc):
        factor = jnp.broadcast_to(winb32[k : k + 1, 0:1], (rows, virt))
        sing[...] += factor * wovb[k].astype(F32)

    local[2].wait()
    fock = foob[...]
    m_first = me * (cw // nocc)
    i, j = iotas(nocc, cw)
    by_i = dot(fock, onehot(i == (j >> ob) + m_first), 0, 0).astype(BF16)
    by_j = dot(fock, onehot(i == (j & (nocc - 1))), 0, 0).astype(BF16)
    p, q = iotas(pairs, nocc)
    take_i = dot(onehot((p >> ob) == q), by_i, 1, 0)
    take_j = dot(onehot((p & (nocc - 1)) == q), by_j, 1, 0)
    p, q = iotas(pairs, cw)
    cmat[0] = jnp.where((p & (nocc - 1)) == (q & (nocc - 1)), take_i, 0.0).astype(BF16)
    cmat[1] = jnp.where((p >> ob) == (q >> ob) + m_first, take_j, 0.0).astype(BF16)

    lax.fori_loop(middle, rounds + LAG, advance, 0)

    local[5].wait()
    local[6].wait()
    others = (nv - 1) * EB
    received(r2s.at[pl.ds(0, others), :], small_recv.at[0])
    received(wos.at[pl.ds(0, nv - 1)], small_recv.at[1])
    held = r2s[...]
    quartic = wos[...].astype(F32).reshape(pairs, cw).astype(BF16)
    add_terms(dot(quartic, held, 1, 1) - dot(cmat[0], held, 1, 1) - dot(cmat[1], held, 1, 1), True)

    side = nx

    def flat(z_at, y_at, x_at):
        return z_at * (ny * nx) + y_at * nx + x_at

    def line(q, at):
        return acc.at[q, :, at] if q % 2 else acc.at[q, :, :, at]

    def here(q):
        return y if q % 2 else x

    def cross(q):
        return x if q % 2 else y

    def to_line(q):
        for offset in range(1, side):
            at = (here(q) + offset) % side
            pltpu.make_async_remote_copy(
                src_ref=line(q, at), dst_ref=near.at[q, offset - 1], send_sem=rs_send.at[q], recv_sem=rs_recv.at[q],
                device_id=(root, flat(zh, at, x) if q % 2 else flat(zh, y, at)), device_id_type=MESH,
            ).start()

    def to_owners(q):
        received(near.at[q], rs_recv.at[q])
        total[q] = line(q, here(q))[...] + jnp.sum(near[q], axis=0)

        def to_owner(i, _):
            z_at, at = (zh + i // side) % 2, (cross(q) + i % side) % side
            pltpu.make_async_remote_copy(
                src_ref=total.at[q, z_at, at], dst_ref=far.at[q, i - 1],
                send_sem=rs_send.at[CHUNKS + q], recv_sem=rs_recv.at[CHUNKS + q],
                device_id=(root, flat(z_at, y, at) if q % 2 else flat(z_at, at, x)), device_id_type=MESH,
            ).start()
            return 0

        lax.fori_loop(1, 2 * side, to_owner, 0)

    ready, over = rounds + LAG, steps + LAG
    for q in range(CHUNKS // 2):
        to_line(q)
    lax.fori_loop(ready, min(ready + UNDER, over), advance, 0)
    for q in range(CHUNKS // 2):
        to_owners(q)
    lax.fori_loop(min(ready + UNDER, over), over, advance, 0)
    for q in range(CHUNKS // 2, CHUNKS):
        to_line(q)
    for q in range(CHUNKS // 2, CHUNKS):
        to_owners(q)

    received(wbuf.at[pl.ds(0, steps), pl.ds(0, LONG)], long_send.at[0])
    received(wbuf.at[pl.ds(0, steps), pl.ds(0, SHARE)], z_send.at[0])
    received(wbuf.at[pl.ds(0, steps), pl.ds(0, HALF)], sib_send.at[0])
    received(r2s.at[pl.ds(0, others), :], small_send.at[0])
    received(wos.at[pl.ds(0, nv - 1)], small_send.at[1])
    for q in range(CHUNKS):
        cols = slice(q * columns, (q + 1) * columns)
        received(far.at[q], rs_recv.at[CHUNKS + q])
        out[:, cols] = total[q, zh, cross(q)] - sing[:, cols] + jnp.sum(far[q], axis=0)
    for q in range(CHUNKS):
        received(near.at[q], rs_send.at[q])
        received(far.at[q], rs_send.at[CHUNKS + q])


def on_device(r2, tau, w, wo, wov, foo, fvv, r1):
    nv = w.shape[1] // w.shape[0]
    side = int(math.isqrt(nv // 2))
    rows, virt, pairs, nocc = wo.shape[0], w.shape[2], tau.shape[2], foo.shape[0]
    cw, columns = wo.shape[1] // nv, virt // CHUNKS
    dma = pltpu.SemaphoreType.DMA
    flops = 2 * nv * EB * EB * pairs * (virt + EB * EB)
    return pl.pallas_call(
        functools.partial(kernel, side, side),
        out_shape=jax.ShapeDtypeStruct((rows, virt), F32),
        in_specs=[pl.BlockSpec(memory_space=pl.ANY)] * 8,
        out_specs=pl.BlockSpec(memory_space=pltpu.VMEM),
        scratch_shapes=[
            pltpu.VMEM((2 * nv, EB, EB, virt // 2), BF16),
            pltpu.VMEM((SLOTS, EB, EB, pairs), BF16),
            pltpu.VMEM((CHUNKS, 2, side, side, rows, columns), F32),
            pltpu.VMEM((CHUNKS, side - 1, 2, side, rows, columns), F32),
            pltpu.VMEM((CHUNKS, 2, side, rows, columns), F32),
            pltpu.VMEM((CHUNKS, 2 * side - 1, rows, columns), F32),
            pltpu.VMEM((nv, pairs, EB * EB), BF16),
            pltpu.VMEM((2, pairs, cw), BF16),
            pltpu.VMEM((nocc, rows, virt), BF16),
            pltpu.VMEM((virt, cw), BF16),
            pltpu.VMEM((nv, rows, cw), BF16),
            pltpu.VMEM((nocc, nocc), BF16),
            pltpu.VMEM((virt, virt), BF16),
            pltpu.VMEM((EB, pairs), BF16),
            pltpu.VMEM((1, nocc), BF16),
            pltpu.VMEM((rows, virt), F32),
            pltpu.VMEM((EB * EB, EB * EB), BF16),
            dma((SLOTS,)), dma((9,)),
            dma((1,)), dma((2 * nv,)), dma((1,)), dma((2 * nv,)), dma((1,)), dma((2 * nv,)),
            dma((2,)), dma((2,)), dma((2 * CHUNKS,)), dma((2 * CHUNKS,)),
        ],
        compiler_params=pltpu.CompilerParams(collective_id=0, has_side_effects=True, vmem_limit_bytes=56 * 2**20),
        cost_estimate=pl.CostEstimate(flops=flops, bytes_accessed=26_000_000, transcendentals=0),
        name="ladder",
    )(r2, tau, w, wo, wov, foo, fvv, r1.reshape(1, -1))


def solution(mesh):
    in_specs = (
        P("virt", "root"),
        P("virt", None, "root"),
        P("virt", None, None),
        P("virt", None),
        P(None, "virt", None),
        P(),
        P(),
        P("root"),
    )
    return jax.shard_map(
        on_device, mesh=mesh, in_specs=in_specs, out_specs=P(("root", "virt"), None), check_vma=False
    )
```

```python
import functools
import math

import jax
import jax.numpy as jnp
from jax import lax
from jax.experimental import pallas as pl
from jax.experimental.pallas import tpu as pltpu
from jax.sharding import PartitionSpec as P

MESH = pl.DeviceIdType.MESH
F32, BF16 = jnp.float32, jnp.bfloat16
EB = 16
HALF = 8
LONG = 5
SHARE = 3
SLOTS = 8
UNDER = 18
CHUNKS = 4
AHEAD = 5
Z_LAG = 12
S_LAG = 5
LAG = Z_LAG + S_LAG


def dot(a, b, ca, cb):
    return lax.dot_general(a, b, (((ca,), (cb,)), ((), ())), preferred_element_type=F32)


def iotas(rows, cols):
    return (lax.broadcasted_iota(jnp.int32, (rows, cols), 0), lax.broadcasted_iota(jnp.int32, (rows, cols), 1))


def onehot(mask):
    return jnp.where(mask, 1.0, 0.0).astype(BF16)


def kernel(
    ny, nx,
    r2, tau, w, wo, wov, foo, fvv, r1,
    out,
    wbuf, tbuf, acc, near, total, far, turned, cmat, wovb, r2s, wos, foob, fvvb, winb, r1b, sing, perm,
    tau_sem, loc_sem, long_send, long_recv, z_send, z_recv, sib_send, sib_recv, small_send, small_recv, rs_send, rs_recv,
):
    nv = 2 * ny * nx
    rounds = nv - 1
    steps = 2 * rounds
    nocc = foo.shape[0]
    pairs = tau.shape[2]
    rows = pairs // nv
    cw = wo.shape[1] // nv
    virt = fvv.shape[0]
    half = virt // 2
    ob = int(math.log2(nocc))
    root, me = lax.axis_index("root"), lax.axis_index("virt")
    zl, c = root // 2, root % 2
    zh, y, x = me // (ny * nx), (me // nx) % ny, me % nx
    sibling = (zl * 2 + 1 - c, me)
    partner = ((1 - zl) * 2 + c, me)

    def peer(j, sign):
        k = (j * 11) % nv
        oz, oy, ox = k // (ny * nx), (k // nx) % ny, k % nx
        v = ((zh + oz) % 2) * (ny * nx) + ((y + sign * oy + ny) % ny) * nx + (x + sign * ox + nx) % nx
        return v, (zl + oz) % 2

    def tau_copy(j):
        v, _ = peer(j, -1)
        return pltpu.make_async_copy(
            tau.at[:, pl.ds(pl.multiple_of(v * EB, EB), EB), :], tbuf.at[j % SLOTS], tau_sem.at[j % SLOTS]
        )

    mine = pl.ds(pl.multiple_of(me * EB, EB), EB)
    my_cols = pl.ds(pl.multiple_of(me * cw, cw), cw)
    local = [
        pltpu.make_async_copy(w.at[:, mine, pl.ds(0, half)], wbuf.at[steps], loc_sem.at[0]),
        pltpu.make_async_copy(wov, wovb, loc_sem.at[1]),
        pltpu.make_async_copy(foo, foob, loc_sem.at[2]),
        pltpu.make_async_copy(fvv, fvvb, loc_sem.at[3]),
        pltpu.make_async_copy(r2.at[:, pl.ds(0, pairs)], winb, loc_sem.at[4]),
        pltpu.make_async_copy(r2.at[:, my_cols], r2s.at[mine, :], loc_sem.at[5]),
        pltpu.make_async_copy(wo.at[:, my_cols], wos.at[me], loc_sem.at[6]),
        pltpu.make_async_copy(r1, r1b, loc_sem.at[7]),
        pltpu.make_async_copy(w.at[:, mine, pl.ds(half, half)], wbuf.at[steps + 1], loc_sem.at[8]),
    ]

    barrier = pltpu.get_barrier_semaphore()

    def greet(j, _):
        v, zd = peer(j, 1)
        pl.semaphore_signal(barrier, inc=1, device_id=(root, v), device_id_type=MESH)

        @pl.when(zd != zl)
        def _():
            pl.semaphore_signal(barrier, inc=1, device_id=(zd * 2 + c, v), device_id_type=MESH)

        return 0

    lax.fori_loop(1, nv, greet, 0)
    for other in (sibling, partner):
        pl.semaphore_signal(barrier, inc=1, device_id=other, device_id_type=MESH)
    for j in range(SLOTS):
        tau_copy(j).start()
    for copy in local:
        copy.start()
    pl.semaphore_wait(barrier, nv - 1 + nv // 2 + 2)

    def small_copies(v):
        cols = pl.ds(pl.multiple_of(v * cw, cw), cw)
        return (
            pltpu.make_async_remote_copy(
                src_ref=r2.at[:, cols], dst_ref=r2s.at[mine, :], send_sem=small_send.at[0], recv_sem=small_recv.at[0],
                device_id=(root, v), device_id_type=MESH,
            ),
            pltpu.make_async_remote_copy(
                src_ref=wo.at[:, cols], dst_ref=wos.at[me], send_sem=small_send.at[1], recv_sem=small_recv.at[1],
                device_id=(root, v), device_id_type=MESH,
            ),
        )

    def send(step, _):
        v, zd = peer(step % rounds + 1, 1)
        first = HALF * c + SHARE * zd
        cols = pl.ds(pl.multiple_of((step // rounds) * half, half), half)
        pltpu.make_async_remote_copy(
            src_ref=w.at[pl.ds(first, LONG), pl.ds(pl.multiple_of(v * EB, EB), EB), cols],
            dst_ref=wbuf.at[step, pl.ds(first, LONG)],
            send_sem=long_send.at[0],
            recv_sem=long_recv.at[step],
            device_id=(zd * 2 + c, v),
            device_id_type=MESH,
        ).start()
        return 0

    def send_small(j, _):
        v, _zd = peer(j, 1)
        for copy in small_copies(v):
            copy.start()
        return 0

    lax.fori_loop(0, rounds, send, 0)
    lax.fori_loop(1, nv, send_small, 0)
    lax.fori_loop(rounds, steps, send, 0)

    i, j = iotas(EB * EB, EB * EB)
    perm[...] = onehot(((i >> 4) == (j & 15)) & ((i & 15) == (j >> 4)))

    local[3].wait()
    local[4].wait()
    i, j = iotas(EB, virt)
    chosen = dot(onehot(j == i + me * EB), fvvb[...], 1, 1).astype(BF16)
    columns = virt // CHUNKS

    def add_terms(value, old):
        for q in range(CHUNKS):
            piece = value[:, q * columns : (q + 1) * columns].reshape(acc.shape[1:])
            acc[q] = acc[q] + piece if old else piece

    add_terms(dot(winb[...], chosen, 0, 0), False)

    def z_copy(j):
        part = wbuf.at[j, pl.ds(HALF * c + LONG * zl, SHARE)]
        return pltpu.make_async_remote_copy(
            src_ref=part, dst_ref=part, send_sem=z_send.at[0], recv_sem=z_recv.at[j], device_id=partner, device_id_type=MESH
        )

    def sib_copy(j):
        part = wbuf.at[j, pl.ds(HALF * c, HALF)]
        return pltpu.make_async_remote_copy(
            src_ref=part, dst_ref=part, send_sem=sib_send.at[0], recv_sem=sib_recv.at[j], device_id=sibling, device_id_type=MESH
        )

    def received(ref, sem):
        pltpu.make_async_copy(ref, ref, sem).wait()

    def prepare(j):
        tau_copy(j).wait()
        block = tbuf[j % SLOTS].reshape(EB * EB, pairs)
        turned[j] = dot(block, perm[...], 0, 0).astype(BF16)

        @pl.when(j + SLOTS < nv)
        def _():
            tau_copy(j + SLOTS).start()

    def compute(j, slot, h):
        weights = wbuf[slot].reshape(EB * EB, half)
        size = pairs // 2
        for part in range(2):
            product = dot(turned[j, pl.ds(part * size, size)], weights, 1, 0)
            for q in range(CHUNKS // 2):
                acc[h * (CHUNKS // 2) + q, part] += product[:, q * columns : (q + 1) * columns].reshape(acc.shape[2:])

    def advance(i, _):
        k, t = i - Z_LAG, i - LAG

        @pl.when(i < steps)
        def _():
            received(wbuf.at[i, pl.ds(HALF * c + SHARE * zl, LONG)], long_recv.at[i])
            z_copy(i).start()

        @pl.when((k >= 0) & (k < steps))
        def _():
            received(wbuf.at[k, pl.ds(HALF * c + LONG * (1 - zl), SHARE)], z_recv.at[k])
            sib_copy(k).start()

        @pl.when(t >= 0)
        def _():
            at = lax.max(t, 0)
            received(wbuf.at[at, pl.ds(HALF * (1 - c), HALF)], sib_recv.at[at])
            compute(at % rounds + 1, at, at // rounds)

        @pl.when(i + AHEAD < nv)
        def _():
            prepare(i + AHEAD)

        return 0

    def prepare_early(j, _):
        prepare(j)
        return 0

    lax.fori_loop(0, AHEAD, prepare_early, 0)
    local[0].wait()
    local[8].wait()
    for h in range(2):
        compute(0, steps + h, h)
    middle = nv // 2
    lax.fori_loop(0, middle, advance, 0)

    local[2].wait()
    fock = foob[...]
    m_first = me * (cw // nocc)
    i, j = iotas(nocc, cw)
    by_i = dot(fock, onehot(i == (j >> ob) + m_first), 0, 0).astype(BF16)
    by_j = dot(fock, onehot(i == (j & (nocc - 1))), 0, 0).astype(BF16)
    p, q = iotas(pairs, nocc)
    take_i = dot(onehot((p >> ob) == q), by_i, 1, 0)
    take_j = dot(onehot((p & (nocc - 1)) == q), by_j, 1, 0)
    p, q = iotas(pairs, cw)
    cmat[0] = jnp.where((p & (nocc - 1)) == (q & (nocc - 1)), take_i, 0.0).astype(BF16)
    cmat[1] = jnp.where((p >> ob) == (q >> ob) + m_first, take_j, 0.0).astype(BF16)

    lax.fori_loop(middle, rounds + LAG, advance, 0)

    local[5].wait()
    local[6].wait()
    others = (nv - 1) * EB
    received(r2s.at[pl.ds(0, others), :], small_recv.at[0])
    received(wos.at[pl.ds(0, nv - 1)], small_recv.at[1])
    held = r2s[...]
    quartic = wos[...].astype(F32).reshape(pairs, cw).astype(BF16)
    add_terms(dot(quartic, held, 1, 1) - dot(cmat[0], held, 1, 1) - dot(cmat[1], held, 1, 1), True)

    side = nx

    def flat(z_at, y_at, x_at):
        return z_at * (ny * nx) + y_at * nx + x_at

    def line(q, at):
        return acc.at[q, :, at] if q % 2 else acc.at[q, :, :, at]

    def here(q):
        return y if q % 2 else x

    def cross(q):
        return x if q % 2 else y

    def to_line(q):
        for offset in range(1, side):
            at = (here(q) + offset) % side
            pltpu.make_async_remote_copy(
                src_ref=line(q, at), dst_ref=near.at[q, offset - 1], send_sem=rs_send.at[q], recv_sem=rs_recv.at[q],
                device_id=(root, flat(zh, at, x) if q % 2 else flat(zh, y, at)), device_id_type=MESH,
            ).start()

    def to_owners(q):
        received(near.at[q], rs_recv.at[q])
        total[q] = line(q, here(q))[...] + jnp.sum(near[q], axis=0)

        def to_owner(i, _):
            z_at, at = (zh + i // side) % 2, (cross(q) + i % side) % side
            pltpu.make_async_remote_copy(
                src_ref=total.at[q, z_at, at], dst_ref=far.at[q, i - 1],
                send_sem=rs_send.at[CHUNKS + q], recv_sem=rs_recv.at[CHUNKS + q],
                device_id=(root, flat(z_at, y, at) if q % 2 else flat(z_at, at, x)), device_id_type=MESH,
            ).start()
            return 0

        lax.fori_loop(1, 2 * side, to_owner, 0)

    ready, over = rounds + LAG, steps + LAG
    for q in range(CHUNKS // 2):
        to_line(q)
    lax.fori_loop(ready, min(ready + UNDER, over), advance, 0)
    for q in range(CHUNKS // 2):
        to_owners(q)
    lax.fori_loop(min(ready + UNDER, over), over, advance, 0)
    for q in range(CHUNKS // 2, CHUNKS):
        to_line(q)

    local[1].wait()
    local[7].wait()
    i, j = iotas(nocc, nocc)
    spread = jnp.where(i == j, jnp.broadcast_to(r1b[...].astype(F32), (nocc, nocc)), 0.0).astype(BF16)
    winb32 = dot(spread, jnp.ones((nocc, 128), BF16), 1, 0)
    sing[...] = jnp.zeros_like(sing)
    for k in range(nocc):
        factor = jnp.broadcast_to(winb32[k : k + 1, 0:1], (rows, virt))
        sing[...] += factor * wovb[k].astype(F32)

    for q in range(CHUNKS // 2, CHUNKS):
        to_owners(q)

    received(wbuf.at[pl.ds(0, steps), pl.ds(0, LONG)], long_send.at[0])
    received(wbuf.at[pl.ds(0, steps), pl.ds(0, SHARE)], z_send.at[0])
    received(wbuf.at[pl.ds(0, steps), pl.ds(0, HALF)], sib_send.at[0])
    received(r2s.at[pl.ds(0, others), :], small_send.at[0])
    received(wos.at[pl.ds(0, nv - 1)], small_send.at[1])
    for q in range(CHUNKS):
        cols = slice(q * columns, (q + 1) * columns)
        received(far.at[q], rs_recv.at[CHUNKS + q])
        out[:, cols] = total[q, zh, cross(q)] - sing[:, cols] + jnp.sum(far[q], axis=0)
    for q in range(CHUNKS):
        received(near.at[q], rs_send.at[q])
        received(far.at[q], rs_send.at[CHUNKS + q])


def on_device(r2, tau, w, wo, wov, foo, fvv, r1):
    nv = w.shape[1] // w.shape[0]
    side = int(math.isqrt(nv // 2))
    rows, virt, pairs, nocc = wo.shape[0], w.shape[2], tau.shape[2], foo.shape[0]
    cw, columns = wo.shape[1] // nv, virt // CHUNKS
    dma = pltpu.SemaphoreType.DMA
    flops = 2 * nv * EB * EB * pairs * (virt + EB * EB)
    return pl.pallas_call(
        functools.partial(kernel, side, side),
        out_shape=jax.ShapeDtypeStruct((rows, virt), F32),
        in_specs=[pl.BlockSpec(memory_space=pl.ANY)] * 8,
        out_specs=pl.BlockSpec(memory_space=pltpu.VMEM),
        scratch_shapes=[
            pltpu.VMEM((2 * nv, EB, EB, virt // 2), BF16),
            pltpu.VMEM((SLOTS, EB, EB, pairs), BF16),
            pltpu.VMEM((CHUNKS, 2, side, side, rows, columns), F32),
            pltpu.VMEM((CHUNKS, side - 1, 2, side, rows, columns), F32),
            pltpu.VMEM((CHUNKS, 2, side, rows, columns), F32),
            pltpu.VMEM((CHUNKS, 2 * side - 1, rows, columns), F32),
            pltpu.VMEM((nv, pairs, EB * EB), BF16),
            pltpu.VMEM((2, pairs, cw), BF16),
            pltpu.VMEM((nocc, rows, virt), BF16),
            pltpu.VMEM((virt, cw), BF16),
            pltpu.VMEM((nv, rows, cw), BF16),
            pltpu.VMEM((nocc, nocc), BF16),
            pltpu.VMEM((virt, virt), BF16),
            pltpu.VMEM((EB, pairs), BF16),
            pltpu.VMEM((1, nocc), BF16),
            pltpu.VMEM((rows, virt), F32),
            pltpu.VMEM((EB * EB, EB * EB), BF16),
            dma((SLOTS,)), dma((9,)),
            dma((1,)), dma((2 * nv,)), dma((1,)), dma((2 * nv,)), dma((1,)), dma((2 * nv,)),
            dma((2,)), dma((2,)), dma((2 * CHUNKS,)), dma((2 * CHUNKS,)),
        ],
        compiler_params=pltpu.CompilerParams(collective_id=0, has_side_effects=True, vmem_limit_bytes=56 * 2**20),
        cost_estimate=pl.CostEstimate(flops=flops, bytes_accessed=26_000_000, transcendentals=0),
        name="ladder",
    )(r2, tau, w, wo, wov, foo, fvv, r1.reshape(1, -1))


def solution(mesh):
    in_specs = (
        P("virt", "root"),
        P("virt", None, "root"),
        P("virt", None, None),
        P("virt", None),
        P(None, "virt", None),
        P(),
        P(),
        P("root"),
    )
    return jax.shard_map(
        on_device, mesh=mesh, in_specs=in_specs, out_specs=P(("root", "virt"), None), check_vma=False
    )
```
